32 devices in a mesh: blen: 4 (over z), tm: 8 (over y, x, core).
Axes of the slice: x: 2, y: 2, z: 4, core: 2. Of those that a mesh axis runs over, the one named last changes fastest.
Arguments:
- model_grid: bfloat16 [256, 2, 512, 512], P(('blen', 'tm')), may hold values from -6 to 6
- vis_values: float32 [2, 16384], P(None, ('blen', 'tm')), may hold values from -6 to 6
- weights: float32 [16384], P(('blen', 'tm')), may hold values from 0.3 to 3
- flags: int32 [16384], P(('blen', 'tm')), may hold values 0 or 1
- uv_frac: float32 [2, 16384], P(None, ('blen', 'tm')), may hold values from 0 to 1
- cell_offset: int32 [2, 16384], P(None, ('blen', 'tm')), may hold values from 3 to 507
- tile_index: int32 [16384, 1], P(('blen', 'tm')), may hold values from 0 to 255; in each aligned block of 512 rows (0 to 511, 512 to 1023, ...) at most 4 rows name the same one
Outputs:
- gradient: float32 [8192, 8192], P(('blen', 'tm'))
- weighted_residual: float32 [2, 16384], P(None, ('blen', 'tm'))
The draws below stay inside these ranges and needn't reach their ends.
Inputs may be any that keep to these rules, and one draw needn't show every extreme that they name: `tile_index`: in the rows of one device no tile is named by more than 4 rows, and some device has a tile named by exactly 4 rows.
All inputs are finite; a program needn't handle non-finite values. No bound on the sum of `flags` on one device may be relied on, other than what follows from the above.
Results may differ from the reference program's by a relative error of at most 0.0095.
Values sent between devices are 32-bit elements; how exact they have to be, the bound alone decides.
No kernel may reach another device: no remote copies, remote signals or barrier semaphores. Data moves between devices by JAX's collectives and lax.ppermute only.
A program may use at most 192 MiB of HBM per device.

```python
import math
from functools import partial
import jax
import jax.numpy as jnp
import numpy as np
from jax import lax

NPIX = 8192
TILE = 512
KSUP = 8
VIS_DEV = 512
NT = 16
NTILES = 256
TVG = 4
MOST = 4
VIS_ALL = 16384
N_BLEN = 4


def plant(result, own_key, least, largest):
    longest = result.shape.index(max(result.shape))
    spots = []
    for shift in (0, 1):
        where = [jax.random.randint(jax.random.fold_in(own_key, axis), (), 0, length) for axis, length in enumerate(result.shape)]
        where[longest] = (where[longest] + shift) % result.shape[longest]
        spots.append(tuple(where))
    return result.at[spots[0]].set(least).at[spots[1]].set(largest)


def block_scale(rng, dims, shards, least, largest):
    def one(position, shards_of):
        draws = jax.random.uniform(jax.random.fold_in(jax.random.fold_in(rng, 6), position), (shards_of,), jnp.float32, least / len(shards), largest / len(shards))
        return jnp.repeat(jnp.exp(draws), dims[position] // shards_of).reshape((-1,) + (1,) * (len(dims) - position - 1))

    factor_of = one(*shards[0])
    for cut in shards[1:]:
        factor_of = factor_of * one(*cut)
    return factor_of


def routed_block(own_key, own, number, rows, count, top, most, lean):
    ranking = jax.random.permutation(own_key, count)
    crowded, usual = portions_of(count, rows * top, most, lean, True), portions_of(count, rows * top, most, lean, False)
    places = jnp.arange(count)

    def named(tallies, offset_by):
        used = int((tallies > 0).sum())
        fixed = max(1, used // 4)
        passed = fixed + (places - fixed + offset_by * (used - fixed)) % max(1, count - fixed)
        return jnp.zeros((count,), jnp.int32).at[ranking[jnp.where(places < fixed, places, passed)]].set(jnp.asarray(tallies, jnp.int32))

    tallies = jnp.where(number % 4 == 0, named(crowded, number // 4), named(usual, number - number // 4 - 1))
    mixed = jax.random.permutation(jax.random.fold_in(own, 3), count)
    giver, taker = mixed[0:count // 2 * 2:2], mixed[1:count // 2 * 2:2]
    slack = jnp.minimum(tallies[giver] - 1, most - tallies[taker]) // 2
    slack = jnp.where((giver == ranking[0]) | (taker == ranking[0]) | (tallies[taker] == 0), 0, jnp.maximum(slack, 0))
    passed = jax.random.randint(jax.random.fold_in(own, 4), (count // 2,), 0, 1 << 20) % (slack + 1)
    tallies = tallies.at[giver].add(-passed).at[taker].add(passed)
    items = jnp.searchsorted(jnp.cumsum(tallies), jnp.arange(rows * top), side="right").astype(jnp.int32)
    grid = items.reshape(top, rows).T
    grid = grid[jax.random.permutation(jax.random.fold_in(own, 1), rows)]
    offset_by = jax.random.randint(jax.random.fold_in(own, 2), (rows, 1), 0, top)
    return jnp.take_along_axis(grid, (jnp.arange(top)[None, :] + offset_by) % top, axis=1)


def portions_of(count, total, most, lean, full):
    portions = [(1 << 20) // math.isqrt(grade ** lean) + 1 for grade in range(1, count + 1)]
    largest = most if full else min(most, max(-(-total // count), total * portions[0] // sum(portions)))
    least = 1 if total - largest >= count - 1 else 0
    given, rest = [largest] + [least] * (count - 1), total - largest - least * (count - 1)
    while rest > 0:
        free = [i for i in range(1, count) if given[i] < largest] or [i for i in range(1, count) if given[i] < most]
        mass, budget = sum([portions[i] for i in free]), rest
        for i in free:
            extra = min(most - given[i], max(1, budget * portions[i] // mass), rest)
            given[i] = given[i] + extra
            rest = rest - extra
    return np.array(given)


def scatter_about(key, extent, width, bound, pieces=(), kind=jnp.bfloat16):
    gain = block_scale(key, extent, pieces, -0.22, 0.18) if pieces else 1.0
    entries = jax.random.normal(key, extent, jnp.float32) * width * gain
    return jnp.minimum(jnp.maximum(entries, -bound), bound).astype(kind)


def setup_inputs(seed: int = 0) -> dict:
    seeds = jax.random.split(jax.random.key(seed), 8)
    model_grid = scatter_about(seeds[0], (NTILES, 2, TILE, TILE), 1.0, 6.0, ((0, 32),))
    vis_values = scatter_about(seeds[1], (2, VIS_ALL), 1.0, 6.0, ((1, 32),), jnp.float32)
    weights = jnp.clip(jnp.exp(math.log(3.0) - 2.3025851 * jax.random.uniform(seeds[2], (VIS_ALL,), jnp.float32) ** block_scale(seeds[2], (VIS_ALL,), ((0, 32),), -0.2, 0.2)), 0.3, 3.0)
    flags = plant((jax.random.randint(seeds[3], (VIS_ALL,), 0, 8) < 7).astype(jnp.int32), jax.random.fold_in(seeds[3], 1), 0, 1)
    uv_frac = jnp.clip(1.0 * jax.random.uniform(seeds[4], (2, VIS_ALL), jnp.float32) ** block_scale(seeds[4], (2, VIS_ALL), ((1, 32),), -0.2, 0.2), 0.0, 1.0)
    cell_offset = plant(jax.random.randint(seeds[5], (2, VIS_ALL), KSUP // 2 - 1, TILE - KSUP // 2), jax.random.fold_in(seeds[5], 1), KSUP // 2 - 1, (TILE - KSUP // 2) - 1).astype(jnp.int32)
    tile_index_keys = jax.random.split(jax.random.fold_in(seeds[6], 1), VIS_ALL // VIS_DEV)
    tile_index_turns = jax.random.permutation(jax.random.fold_in(seeds[6], 3), VIS_ALL // VIS_DEV)
    tile_index = jax.vmap(lambda own, number: routed_block(jax.random.fold_in(seeds[6], 2), own, number, VIS_DEV, NTILES, 1, MOST, 2))(tile_index_keys, tile_index_turns).reshape((VIS_ALL, 1))
    return {"model_grid": model_grid, "vis_values": vis_values, "weights": weights, "flags": flags, "uv_frac": uv_frac, "cell_offset": cell_offset, "tile_index": tile_index}


kernel_scale = 0.5


def kernel_taps(frac):
    tap_steps = jnp.arange(KSUP, dtype=jnp.int32) - (KSUP // 2 - 1)
    distance = tap_steps.astype(jnp.float32)[None, :] - frac[:, None]
    rounded = jnp.exp(-kernel_scale * distance * distance).astype(jnp.bfloat16)
    return lax.optimization_barrier(rounded).astype(jnp.float32)


def patch_at(model_grid, tile_id, corner_v, corner_u):
    anchor = jnp.zeros((), jnp.int32)
    return lax.dynamic_slice(model_grid, (tile_id, anchor, corner_v, corner_u), (1, 2, KSUP, KSUP))[0]


def reference(model_grid, vis_values, weights, flags, uv_frac, cell_offset, tile_index):
    tile_ids = tile_index[:, 0].astype(jnp.int32)
    corner_u = (cell_offset[0] - (KSUP // 2 - 1)).astype(jnp.int32)
    corner_v = (cell_offset[1] - (KSUP // 2 - 1)).astype(jnp.int32)
    taps_u = kernel_taps(uv_frac[0])
    taps_v = kernel_taps(uv_frac[1])
    patches = jax.vmap(partial(patch_at, model_grid))(tile_ids, corner_v, corner_u).astype(jnp.float32)
    predicted = jnp.einsum('qj,qcji,qi->qc', taps_v, patches, taps_u)
    weighted = weights * flags.astype(jnp.float32)
    residual = weighted[:, None] * (predicted - vis_values.T)
    spread = (residual[:, :, None] * taps_u[:, None, :]).astype(jnp.bfloat16)
    spread = lax.optimization_barrier(spread).astype(jnp.float32)
    deposits = taps_v[:, None, :, None] * spread[:, :, None, :]
    span = jnp.arange(KSUP, dtype=jnp.int32)
    row_cells = corner_v[:, None, None, None] + span[None, None, :, None]
    col_cells = corner_u[:, None, None, None] + span[None, None, None, :]
    parts = jnp.arange(2, dtype=jnp.int32)[None, :, None, None]
    adjoint = jnp.zeros((NTILES, 2, TILE, TILE), jnp.float32)
    adjoint = adjoint.at[tile_ids[:, None, None, None], parts, row_cells, col_cells].add(deposits)
    uv_grid = adjoint.reshape(N_BLEN, NT, TVG, 2, TILE, TILE).transpose(3, 1, 5, 0, 2, 4).reshape(2, NPIX, NPIX)
    sky_field = jnp.fft.ifft2(lax.complex(uv_grid[0], uv_grid[1]))
    gradient = jnp.real(sky_field) * NPIX
    return gradient.astype(jnp.float32), residual.T
```

```python
import math

import jax
import jax.numpy as jnp
from jax import lax
from jax.experimental import pallas as pl
from jax.experimental.pallas import tpu as pltpu
from jax.sharding import PartitionSpec as P

NPIX = 8192
KSUP = 8
NT = 16
TVG = 4
MOST = 4
FIELDS = 8
KEPT = 4

AXES = ("blen", "tm")
f32 = jnp.float32
bf16 = jnp.bfloat16
i32 = jnp.int32
NT_DIMS = (((1,), (1,)), ((), ()))
NN_DIMS = (((1,), (0,)), ((), ()))
MIB = 1 << 20


def params(mib):
    return pltpu.CompilerParams(vmem_limit_bytes=mib * MIB)


def split3(x):
    hi = x.astype(bf16)
    rest = x - hi.astype(f32)
    mid = rest.astype(bf16)
    low = (rest - mid.astype(f32)).astype(bf16)
    return hi, mid, low


def tap_block(cells_i, cells_f, offset_row, frac_row):
    first = offset_row.astype(i32) - (KSUP // 2 - 1)
    steps = cells_i - first
    dist = (cells_f - offset_row) - frac_row
    value = jnp.exp(-0.5 * dist * dist)
    inside = (steps >= 0) & (steps < KSUP)
    return jnp.where(inside, value, 0.0).astype(bf16)


def pack_body(tile_col, tile_row, fields, packed, slots, *, devices, per_dev):
    n = tile_row.shape[1]
    t_row = tile_row[...]
    earlier = lax.broadcasted_iota(i32, (n, n), 0) < lax.broadcasted_iota(i32, (n, n), 1)
    same = (tile_col[...] == t_row) & earlier
    rank = jnp.sum(same.astype(f32), axis=0, keepdims=True).astype(i32)
    owner = t_row // per_dev
    local = t_row - owner * per_dev
    slots[...] = rank
    owners = lax.broadcasted_iota(i32, (devices, n), 0) == owner
    places = MOST * per_dev
    hot = (lax.broadcasted_iota(i32, (places, n), 0) == rank * per_dev + local)
    hot = hot.astype(f32).astype(bf16)
    packed[...] = jnp.zeros(packed.shape, f32)
    for f in range(FIELDS - 1):
        spread = jnp.where(owners, fields[f : f + 1, :], 0.0)
        total = jnp.zeros((devices, places), f32)
        for part in split3(spread):
            total = total + lax.dot_general(part, hot, NT_DIMS, preferred_element_type=f32)
        for k in range(MOST):
            at = (k * FIELDS + f) * per_dev
            packed[:, at : at + per_dev] = total[:, k * per_dev : (k + 1) * per_dev]


def unpack_body(recv, pos, rest, *, devices, per_dev):
    turned = recv[...].T
    span = FIELDS * per_dev
    rows = jnp.concatenate([turned[k * span : (k + 1) * span, :] for k in range(MOST)], axis=1)
    for l in range(per_dev):
        for f in range(KEPT):
            pos[l, f : f + 1, :] = rows[f * per_dev + l : f * per_dev + l + 1, :]
            g = f + KEPT
            rest[l, f : f + 1, :] = rows[g * per_dev + l : g * per_dev + l + 1, :]


def predict_body(model, pos, rest, res):
    side = model.shape[2]
    lanes = pos.shape[2]
    cells_i = lax.broadcasted_iota(i32, (side, lanes), 0)
    cells_f = cells_i.astype(f32)
    ku = tap_block(cells_i, cells_f, pos[0, 0:1, :], pos[0, 2:3, :])
    kv = tap_block(cells_i, cells_f, pos[0, 1:2, :], pos[0, 3:4, :]).astype(f32)
    for c in range(2):
        rows = lax.dot_general(model[0, c], ku, NN_DIMS, preferred_element_type=f32)
        predicted = jnp.sum(rows * kv, axis=0, keepdims=True)
        res[0, c : c + 1, :] = rest[0, 2:3, :] * (predicted - rest[0, c : c + 1, :])


def columns_body(pos, res, turn_u, rot, out, kv_all, up_all, *, lanes):
    side = turn_u.shape[1]
    rows2 = turn_u.shape[0]
    rows = rows2 // 2
    short = side // NT
    cells_i = lax.broadcasted_iota(i32, (side, lanes), 0)
    cells_f = cells_i.astype(f32)
    perm_i = (cells_i % short) * NT + cells_i // short
    perm_f = perm_i.astype(f32)

    def step(tu, carry):
        at = pl.multiple_of(tu * lanes, lanes)
        p = pos[0, tu, 0]
        r = res[0, tu, 0]
        ku = tap_block(cells_i, cells_f, p[0:1], p[2:3])
        kv_all[:, pl.ds(at, lanes)] = tap_block(perm_i, perm_f, p[1:2], p[3:4])
        v = lax.dot_general(turn_u[...], ku, NN_DIMS, preferred_element_type=f32)
        r_re = r[0:1] * (1.0 / NPIX)
        r_im = r[1:2] * (1.0 / NPIX)
        cos_t = rot[0, :, pl.ds(at, lanes)]
        sin_t = rot[1, :, pl.ds(at, lanes)]
        c_re = (r_re * cos_t - r_im * sin_t)[None]
        c_im = (r_re * sin_t + r_im * cos_t)[None]
        v_re = v[:rows].reshape(rows // NT, NT, lanes)
        v_im = v[rows:].reshape(rows // NT, NT, lanes)
        u_re = (c_re * v_re - c_im * v_im).reshape(rows, lanes)
        u_im = (c_re * v_im + c_im * v_re).reshape(rows, lanes)
        up_all[0:rows, pl.ds(at, lanes)] = u_re.astype(bf16)
        up_all[rows:rows2, pl.ds(at, lanes)] = u_im.astype(bf16)
        return carry

    lax.fori_loop(0, NT, step, 0)
    ft = lax.dot_general(kv_all[...], up_all[...], NT_DIMS, preferred_element_type=f32)
    out[...] = ft.astype(bf16).reshape(NT, short, rows2)


def fft_pos(z, real_only=False):
    n = len(z)
    if n == 1:
        return z
    even = fft_pos(z[0::2])
    odd = fft_pos(z[1::2])
    low, high = [], []
    for k in range(n // 2):
        o_re, o_im = odd[k]
        if k == 0:
            t_re, t_im = o_re, o_im
        elif 4 * k == n:
            t_re, t_im = -o_im, o_re
        else:
            c, s = math.cos(2 * math.pi * k / n), math.sin(2 * math.pi * k / n)
            t_re = o_re * c - o_im * s
            t_im = None if real_only else o_re * s + o_im * c
        e_re, e_im = even[k]
        if real_only:
            low.append(e_re + t_re)
            high.append(e_re - t_re)
        else:
            low.append((e_re + t_re, e_im + t_im))
            high.append((e_re - t_re, e_im - t_im))
    return low + high


def rows_body(ft, turn_v, twist, out, mid, real, *, block):
    b1 = ft.shape[1]
    rows2 = ft.shape[2]
    rows = rows2 // 2
    at = pl.program_id(0)
    for b0 in range(NT):
        both = lax.dot_general(
            turn_v[...].reshape(2 * block, b1), ft[b0], NN_DIMS, preferred_element_type=f32
        )
        p, q = both[:block], both[block:]
        a_re = p[:, :rows] - q[:, rows:]
        a_im = p[:, rows:] + q[:, :rows]
        if b0 > 0:
            c = twist[0, :, b0 : b0 + 1]
            s = twist[1, :, b0 : b0 + 1]
            a_re, a_im = a_re * c - a_im * s, a_re * s + a_im * c
        mid[0, b0] = a_re
        mid[1, b0] = a_im

    def group(g, carry):
        r0 = pl.multiple_of(g * 8, 8)
        z = [(mid[0, b0, pl.ds(r0, 8), :], mid[1, b0, pl.ds(r0, 8), :]) for b0 in range(NT)]
        x = fft_pos(z, True)
        for n0 in range(NT):
            real[n0, pl.ds(r0, 8), :] = x[n0]
        return carry

    lax.fori_loop(0, block // 8, group, 0)
    for n0 in range(NT):
        off = pl.multiple_of(n0 * b1 + at * block, block)
        out[:, pl.ds(off, block)] = real[n0].T


def own_body(res, tile_row, lane_row, out):
    tiles = res.shape[1]
    lanes = res.shape[2]
    n = tile_row.shape[1]
    hot = lax.broadcasted_iota(i32, (lanes, n), 0) == lane_row[...]
    hot = hot.astype(f32).astype(bf16)
    mine = lax.broadcasted_iota(i32, (tiles, n), 0) == tile_row[...]
    for c in range(2):
        total = jnp.zeros((tiles, n), f32)
        for part in split3(res[c]):
            total = total + lax.dot_general(part, hot, NN_DIMS, preferred_element_type=f32)
        out[c : c + 1, :] = jnp.sum(jnp.where(mine, total, 0.0), axis=0, keepdims=True)


def cos_sin(product, period):
    angle = (2.0 * math.pi / period) * (product % period).astype(f32)
    return jnp.cos(angle), jnp.sin(angle)


def to_all(x, devices):
    sent = jnp.broadcast_to(x[None], (devices,) + x.shape)
    return lax.all_to_all(sent, AXES, split_axis=0, concat_axis=0, tiled=True)


def on_device(model_grid, vis_values, weights, flags, uv_frac, cell_offset, tile_index):
    devices = lax.axis_size("blen") * lax.axis_size("tm")
    me = lax.axis_index("blen") * lax.axis_size("tm") + lax.axis_index("tm")
    per_dev = model_grid.shape[0]
    side = model_grid.shape[2]
    n = weights.shape[0]
    ntiles = per_dev * devices
    lanes = devices * MOST
    rows = NPIX // devices
    short = side // NT
    call = pl.pallas_call
    shape = jax.ShapeDtypeStruct

    tile_row = tile_index.reshape(1, n)
    weighted = weights * flags.astype(f32)
    fields = jnp.concatenate(
        [
            cell_offset.astype(f32),
            uv_frac,
            vis_values,
            weighted[None],
            jnp.zeros((1, n), f32),
        ]
    )
    width = MOST * FIELDS * per_dev
    packed, rank = call(
        lambda *refs: pack_body(*refs, devices=devices, per_dev=per_dev),
        out_shape=(shape((devices, width), f32), shape((1, n), i32)),
        name="pack",
    )(tile_index, tile_row, fields)
    recv = lax.all_to_all(packed, AXES, split_axis=0, concat_axis=0, tiled=True)
    pos, rest = call(
        lambda *refs: unpack_body(*refs, devices=devices, per_dev=per_dev),
        out_shape=(shape((per_dev, KEPT, lanes), f32), shape((per_dev, KEPT, lanes), f32)),
        name="unpack",
    )(recv)
    all_pos = to_all(pos, devices).reshape(NT // TVG, NT, TVG, KEPT, lanes)
    res = call(
        predict_body,
        grid=(per_dev,),
        in_specs=[
            pl.BlockSpec((1, 2, side, side), lambda l: (l, 0, 0, 0)),
            pl.BlockSpec((1, KEPT, lanes), lambda l: (l, 0, 0)),
            pl.BlockSpec((1, KEPT, lanes), lambda l: (l, 0, 0)),
        ],
        out_specs=pl.BlockSpec((1, 2, lanes), lambda l: (l, 0, 0)),
        out_shape=shape((per_dev, 2, lanes), f32),
        compiler_params=params(32),
        name="predict",
    )(model_grid, pos, rest)
    all_res = to_all(res, devices)
    weighted_residual = call(
        own_body,
        out_shape=shape((2, n), f32),
        name="own",
    )(
        all_res.reshape(ntiles, 2, lanes).transpose(1, 0, 2),
        tile_row,
        rank * devices + me,
    )

    image_rows = me * rows + jnp.arange(rows, dtype=i32)
    cells = jnp.arange(side, dtype=i32)
    turn_u = jnp.concatenate(cos_sin(image_rows[:, None] * cells[None, :], NPIX)).astype(bf16)
    lane_tile = jnp.arange(NT * lanes, dtype=i32) // lanes
    rot = jnp.stack(cos_sin(jnp.arange(NT, dtype=i32)[:, None] * lane_tile[None, :], NT))
    columns = call(
        lambda *refs: columns_body(*refs, lanes=lanes),
        grid=(NT,),
        in_specs=[
            pl.BlockSpec((1, NT, 1, KEPT, lanes), lambda t: (t // TVG, 0, t % TVG, 0, 0)),
            pl.BlockSpec((1, NT, 1, 2, lanes), lambda t: (t // TVG, 0, t % TVG, 0, 0)),
            pl.BlockSpec((2 * rows, side), lambda t: (0, 0)),
            pl.BlockSpec((2, NT, NT * lanes), lambda t: (0, 0, 0)),
        ],
        out_specs=pl.BlockSpec((NT, short, 2 * rows), lambda t: (0, t, 0)),
        out_shape=shape((NT, side, 2 * rows), bf16),
        scratch_shapes=[
            pltpu.VMEM((side, NT * lanes), bf16),
            pltpu.VMEM((2 * rows, NT * lanes), bf16),
        ],
        compiler_params=params(48),
        name="columns",
    )(all_pos, all_res.reshape(NT // TVG, NT, TVG, 2, lanes), turn_u, rot)

    block = 128
    turn_v = jnp.stack(cos_sin(cells[:, None] * cells[None, :], side)).astype(bf16)
    twist = jnp.stack(cos_sin(cells[:, None] * jnp.arange(NT, dtype=i32)[None, :], NPIX))
    gradient = call(
        lambda *refs: rows_body(*refs, block=block),
        grid=(side // block,),
        in_specs=[
            pl.BlockSpec((NT, side, 2 * rows), lambda b: (0, 0, 0)),
            pl.BlockSpec((2, block, side), lambda b: (0, b, 0)),
            pl.BlockSpec((2, block, NT), lambda b: (0, b, 0)),
        ],
        out_specs=pl.BlockSpec((rows, NPIX), lambda b: (0, 0)),
        out_shape=shape((rows, NPIX), f32),
        scratch_shapes=[
            pltpu.VMEM((2, NT, block, rows), f32),
            pltpu.VMEM((NT, block, rows), f32),
        ],
        compiler_params=params(56),
        name="rows",
    )(columns, turn_v, twist)
    return (gradient, weighted_residual)


def solution(mesh):
    in_specs = (
        P(AXES, None, None, None),
        P(None, AXES),
        P(AXES),
        P(AXES),
        P(None, AXES),
        P(None, AXES),
        P(AXES, None),
    )
    out_specs = (P(AXES, None), P(None, AXES))
    return jax.shard_map(
        on_device, mesh=mesh, in_specs=in_specs, out_specs=out_specs, check_vma=False
    )
```

```python
import math

import jax
import jax.numpy as jnp
from jax import lax
from jax.experimental import pallas as pl
from jax.experimental.pallas import tpu as pltpu
from jax.sharding import PartitionSpec as P

NPIX = 8192
KSUP = 8
NT = 16
TVG = 4
MOST = 4
FIELDS = 8
KEPT = 4
CELLS = 16

AXES = ("blen", "tm")
f32 = jnp.float32
bf16 = jnp.bfloat16
i32 = jnp.int32
NT_DIMS = (((1,), (1,)), ((), ()))
NN_DIMS = (((1,), (0,)), ((), ()))
MIB = 1 << 20


def params(mib):
    return pltpu.CompilerParams(vmem_limit_bytes=mib * MIB)


def split3(x):
    hi = x.astype(bf16)
    rest = x - hi.astype(f32)
    mid = rest.astype(bf16)
    low = (rest - mid.astype(f32)).astype(bf16)
    return hi, mid, low


def tap_block(cells_i, cells_f, offset_row, frac_row):
    first = offset_row.astype(i32) - (KSUP // 2 - 1)
    steps = cells_i - first
    dist = (cells_f - offset_row) - frac_row
    value = jnp.exp(-0.5 * dist * dist)
    inside = (steps >= 0) & (steps < KSUP)
    return jnp.where(inside, value, 0.0).astype(bf16)


def pack_body(tile_col, tile_row, fields, packed, slots, *, devices, per_dev):
    n = tile_row.shape[1]
    t_row = tile_row[...]
    earlier = lax.broadcasted_iota(i32, (n, n), 0) < lax.broadcasted_iota(i32, (n, n), 1)
    same = (tile_col[...] == t_row) & earlier
    rank = jnp.sum(same.astype(f32), axis=0, keepdims=True).astype(i32)
    owner = t_row // per_dev
    local = t_row - owner * per_dev
    slots[...] = rank
    owners = lax.broadcasted_iota(i32, (devices, n), 0) == owner
    places = MOST * per_dev
    hot = (lax.broadcasted_iota(i32, (places, n), 0) == rank * per_dev + local)
    hot = hot.astype(f32).astype(bf16)
    packed[...] = jnp.zeros(packed.shape, f32)
    for f in range(FIELDS - 1):
        spread = jnp.where(owners, fields[f : f + 1, :], 0.0)
        total = jnp.zeros((devices, places), f32)
        for part in split3(spread):
            total = total + lax.dot_general(part, hot, NT_DIMS, preferred_element_type=f32)
        for k in range(MOST):
            at = (k * FIELDS + f) * per_dev
            packed[:, at : at + per_dev] = total[:, k * per_dev : (k + 1) * per_dev]


def unpack_body(recv, pos, rest, *, devices, per_dev):
    turned = recv[...].T
    span = FIELDS * per_dev
    rows = jnp.concatenate([turned[k * span : (k + 1) * span, :] for k in range(MOST)], axis=1)
    for l in range(per_dev):
        for f in range(KEPT):
            pos[l, f : f + 1, :] = rows[f * per_dev + l : f * per_dev + l + 1, :]
            g = f + KEPT
            rest[l, f : f + 1, :] = rows[g * per_dev + l : g * per_dev + l + 1, :]


def predict_body(model, pos, rest, res):
    side = model.shape[2]
    lanes = pos.shape[2]
    cells_i = lax.broadcasted_iota(i32, (side, lanes), 0)
    cells_f = cells_i.astype(f32)
    ku = tap_block(cells_i, cells_f, pos[0, 0:1, :], pos[0, 2:3, :])
    kv = tap_block(cells_i, cells_f, pos[0, 1:2, :], pos[0, 3:4, :]).astype(f32)
    for c in range(2):
        rows = lax.dot_general(model[0, c], ku, NN_DIMS, preferred_element_type=f32)
        predicted = jnp.sum(rows * kv, axis=0, keepdims=True)
        res[0, c : c + 1, :] = rest[0, 2:3, :] * (predicted - rest[0, c : c + 1, :])


def pattern(first, frac):
    cells = lax.broadcasted_iota(i32, (CELLS, first.shape[1]), 0)
    k = (cells - first) & (CELLS - 1)
    dist = (k - (KSUP // 2 - 1)).astype(f32) - frac
    value = jnp.where(k < KSUP, jnp.exp(-0.5 * dist * dist), 0.0).astype(bf16)
    return value, ((first + k) >> 4).astype(f32).astype(bf16)


def dense(value, where, side):
    zero = jnp.zeros_like(value)
    blocks = [jnp.where(where == jnp.bfloat16(b), value, zero) for b in range(side // CELLS)]
    return jnp.concatenate(blocks, axis=0)


def columns_body(pos, res, turn_u, rot, out, kv_all, up_all, *, lanes):
    side = turn_u.shape[1]
    rows2 = turn_u.shape[0]
    rows = rows2 // 2
    per = max(1, 512 // lanes)
    span = per * lanes
    for step in range(NT // per):
        at = step * span
        p = jnp.concatenate([pos[0, step * per + i, 0] for i in range(per)], axis=1)
        r = jnp.concatenate([res[0, step * per + i, 0] for i in range(per)], axis=1)
        first = p[0:2].astype(i32) - (KSUP // 2 - 1)
        ku = dense(*pattern(first[0:1], p[2:3]), side)
        kv_all[:, at : at + span] = dense(*pattern(first[1:2], p[3:4]), side)
        v = lax.dot_general(turn_u[...], ku, NN_DIMS, preferred_element_type=f32)
        r_re = r[0:1] * (1.0 / NPIX)
        r_im = r[1:2] * (1.0 / NPIX)
        cos_t = rot[0, :, at : at + span]
        sin_t = rot[1, :, at : at + span]
        c_re = (r_re * cos_t - r_im * sin_t)[None]
        c_im = (r_re * sin_t + r_im * cos_t)[None]
        v_re = v[:rows].reshape(rows // NT, NT, span)
        v_im = v[rows:].reshape(rows // NT, NT, span)
        u_re = (c_re * v_re - c_im * v_im).reshape(rows, span)
        u_im = (c_re * v_im + c_im * v_re).reshape(rows, span)
        up_all[0:rows, at : at + span] = u_re.astype(bf16)
        up_all[rows:rows2, at : at + span] = u_im.astype(bf16)
    ft = lax.dot_general(kv_all[...], up_all[...], NT_DIMS, preferred_element_type=f32)
    out[0] = ft.astype(bf16)


def fft_pos(z, real_only=False):
    n = len(z)
    if n == 1:
        return z
    even = fft_pos(z[0::2])
    odd = fft_pos(z[1::2])
    low, high = [], []
    for k in range(n // 2):
        o_re, o_im = odd[k]
        if k == 0:
            t_re, t_im = o_re, o_im
        elif 4 * k == n:
            t_re, t_im = -o_im, o_re
        else:
            c, s = math.cos(2 * math.pi * k / n), math.sin(2 * math.pi * k / n)
            t_re = o_re * c - o_im * s
            t_im = None if real_only else o_re * s + o_im * c
        e_re, e_im = even[k]
        if real_only:
            low.append(e_re + t_re)
            high.append(e_re - t_re)
        else:
            low.append((e_re + t_re, e_im + t_im))
            high.append((e_re - t_re, e_im - t_im))
    return low + high


def rows_body(ft, turn_v, twist, out, turned, *flips, steps):
    side = turn_v.shape[0]
    rows = ft.shape[2] // 2
    part = ft.shape[1]
    width = flips[0].shape[1]
    g = pl.program_id(0)

    @pl.when(g < steps)
    def _():
        for j in range(part // 16):
            r0 = j * 16
            tc = twist[0, r0 : r0 + 16, :]
            ts = twist[1, r0 : r0 + 16, :]
            at = pl.multiple_of(g * part + r0, 16)
            for h in range(rows // width):
                c0 = h * width
                z = [
                    (
                        ft[t, r0 : r0 + 16, c0 : c0 + width].astype(f32),
                        ft[t, r0 : r0 + 16, rows + c0 : rows + c0 + width].astype(f32),
                    )
                    for t in range(NT)
                ]
                x = fft_pos(z)
                for n0 in range(NT):
                    re, im = x[n0]
                    if n0 > 0:
                        c = tc[:, n0 : n0 + 1]
                        s = ts[:, n0 : n0 + 1]
                        re, im = re * c - im * s, re * s + im * c
                    turned[n0, pl.ds(at, 16), c0 : c0 + width] = re.astype(bf16)
                    turned[n0, pl.ds(at + side, 16), c0 : c0 + width] = im.astype(bf16)

    @pl.when(g == steps)
    def _():
        for n0 in range(NT):
            x = lax.dot_general(turn_v[...], turned[n0], NN_DIMS, preferred_element_type=f32)
            for h in range(rows // width):
                flips[h][pl.ds(n0, side, stride=NT), :] = x[:, h * width : (h + 1) * width]

    @pl.when(g > steps)
    def _():
        cols = out.shape[1]
        at = pl.multiple_of((g - steps - 1) * cols, cols)
        for h in range(rows // width):
            out[h * width : (h + 1) * width, :] = flips[h][pl.ds(at, cols), :].T


def own_body(res, tile_row, lane_row, out):
    tiles = res.shape[1]
    lanes = res.shape[2]
    n = tile_row.shape[1]
    hot = lax.broadcasted_iota(i32, (lanes, n), 0) == lane_row[...]
    hot = hot.astype(f32).astype(bf16)
    mine = lax.broadcasted_iota(i32, (tiles, n), 0) == tile_row[...]
    for c in range(2):
        total = jnp.zeros((tiles, n), f32)
        for part in split3(res[c]):
            total = total + lax.dot_general(part, hot, NN_DIMS, preferred_element_type=f32)
        out[c : c + 1, :] = jnp.sum(jnp.where(mine, total, 0.0), axis=0, keepdims=True)


def cos_sin(product, period):
    angle = (2.0 * math.pi / period) * (product % period).astype(f32)
    return jnp.cos(angle), jnp.sin(angle)


def to_all(x, devices):
    sent = jnp.broadcast_to(x[None], (devices,) + x.shape)
    return lax.all_to_all(sent, AXES, split_axis=0, concat_axis=0, tiled=True)


def on_device(model_grid, vis_values, weights, flags, uv_frac, cell_offset, tile_index):
    devices = lax.axis_size("blen") * lax.axis_size("tm")
    me = lax.axis_index("blen") * lax.axis_size("tm") + lax.axis_index("tm")
    per_dev = model_grid.shape[0]
    side = model_grid.shape[2]
    n = weights.shape[0]
    ntiles = per_dev * devices
    lanes = devices * MOST
    rows = NPIX // devices
    call = pl.pallas_call
    shape = jax.ShapeDtypeStruct

    tile_row = tile_index.reshape(1, n)
    weighted = weights * flags.astype(f32)
    fields = jnp.concatenate(
        [
            cell_offset.astype(f32),
            uv_frac,
            vis_values,
            weighted[None],
            jnp.zeros((1, n), f32),
        ]
    )
    width = MOST * FIELDS * per_dev
    packed, rank = call(
        lambda *refs: pack_body(*refs, devices=devices, per_dev=per_dev),
        out_shape=(shape((devices, width), f32), shape((1, n), i32)),
        name="pack",
    )(tile_index, tile_row, fields)
    recv = lax.all_to_all(packed, AXES, split_axis=0, concat_axis=0, tiled=True)
    pos, rest = call(
        lambda *refs: unpack_body(*refs, devices=devices, per_dev=per_dev),
        out_shape=(shape((per_dev, KEPT, lanes), f32), shape((per_dev, KEPT, lanes), f32)),
        name="unpack",
    )(recv)
    all_pos = to_all(pos, devices)
    res = call(
        predict_body,
        grid=(per_dev,),
        in_specs=[
            pl.BlockSpec((1, 2, side, side), lambda l: (l, 0, 0, 0)),
            pl.BlockSpec((1, KEPT, lanes), lambda l: (l, 0, 0)),
            pl.BlockSpec((1, KEPT, lanes), lambda l: (l, 0, 0)),
        ],
        out_specs=pl.BlockSpec((1, 2, lanes), lambda l: (l, 0, 0)),
        out_shape=shape((per_dev, 2, lanes), f32),
        compiler_params=params(32),
        name="predict",
    )(model_grid, pos, rest)
    res, all_pos = lax.optimization_barrier((res, all_pos))
    all_pos = all_pos.reshape(NT // TVG, NT, TVG, KEPT, lanes)
    all_res = to_all(res, devices)
    weighted_residual = call(
        own_body,
        out_shape=shape((2, n), f32),
        name="own",
    )(
        all_res.reshape(ntiles, 2, lanes).transpose(1, 0, 2),
        tile_row,
        rank * devices + me,
    )

    image_rows = me * rows + jnp.arange(rows, dtype=i32)
    cells = jnp.arange(side, dtype=i32)
    turn_u = jnp.concatenate(cos_sin(image_rows[:, None] * cells[None, :], NPIX)).astype(bf16)
    lane_tile = jnp.arange(NT * lanes, dtype=i32) // lanes
    rot = jnp.stack(cos_sin(jnp.arange(NT, dtype=i32)[:, None] * lane_tile[None, :], NT))
    columns = call(
        lambda *refs: columns_body(*refs, lanes=lanes),
        grid=(NT,),
        in_specs=[
            pl.BlockSpec((1, NT, 1, KEPT, lanes), lambda t: (t // TVG, 0, t % TVG, 0, 0)),
            pl.BlockSpec((1, NT, 1, 2, lanes), lambda t: (t // TVG, 0, t % TVG, 0, 0)),
            pl.BlockSpec((2 * rows, side), lambda t: (0, 0)),
            pl.BlockSpec((2, NT, NT * lanes), lambda t: (0, 0, 0)),
        ],
        out_specs=pl.BlockSpec((1, side, 2 * rows), lambda t: (t, 0, 0)),
        out_shape=shape((NT, side, 2 * rows), bf16),
        scratch_shapes=[
            pltpu.VMEM((side, NT * lanes), bf16),
            pltpu.VMEM((2 * rows, NT * lanes), bf16),
        ],
        compiler_params=params(48),
        name="columns",
    )(all_pos, all_res.reshape(NT // TVG, NT, TVG, 2, lanes), turn_u, rot)

    steps = 8
    part = side // steps
    width = min(128, rows)
    wide = 512
    cos_v, sin_v = cos_sin(cells[:, None] * cells[None, :], side)
    turn_v = jnp.concatenate([cos_v, -sin_v], axis=1).astype(bf16)
    twist = jnp.stack(cos_sin(cells[:, None] * jnp.arange(NT, dtype=i32)[None, :], NPIX))
    last = steps - 1
    gradient = call(
        lambda *refs: rows_body(*refs, steps=steps),
        grid=(steps + 1 + NPIX // wide,),
        in_specs=[
            pl.BlockSpec((NT, part, 2 * rows), lambda g: (0, jnp.minimum(g, last), 0)),
            pl.BlockSpec((side, 2 * side), lambda g: (0, 0)),
            pl.BlockSpec((2, part, NT), lambda g: (0, jnp.minimum(g, last), 0)),
        ],
        out_specs=pl.BlockSpec((rows, wide), lambda g: (0, jnp.maximum(g - steps - 1, 0))),
        out_shape=shape((rows, NPIX), f32),
        scratch_shapes=[pltpu.VMEM((NT, 2 * side, rows), bf16)]
        + [pltpu.VMEM((NPIX, width), f32)] * (rows // width),
        compiler_params=params(48),
        name="rows",
    )(columns, turn_v, twist)
    return (gradient, weighted_residual)


def solution(mesh):
    in_specs = (
        P(AXES, None, None, None),
        P(None, AXES),
        P(AXES),
        P(AXES),
        P(None, AXES),
        P(None, AXES),
        P(AXES, None),
    )
    out_specs = (P(AXES, None), P(None, AXES))
    return jax.shard_map(
        on_device, mesh=mesh, in_specs=in_specs, out_specs=out_specs, check_vma=False
    )
```

```python
import math

import jax
import jax.numpy as jnp
from jax import lax
from jax.experimental import pallas as pl
from jax.experimental.pallas import tpu as pltpu
from jax.sharding import PartitionSpec as P

NPIX = 8192
KSUP = 8
NT = 16
TVG = 4
MOST = 4
FIELDS = 8
USED = 7
SENT = 6
CELLS = 16
CHUNK = 256

AXES = ("blen", "tm")
f32 = jnp.float32
bf16 = jnp.bfloat16
i32 = jnp.int32
NT_DIMS = (((1,), (1,)), ((), ()))
NN_DIMS = (((1,), (0,)), ((), ()))
MIB = 1 << 20


def params(mib):
    return pltpu.CompilerParams(vmem_limit_bytes=mib * MIB)


def split3(x):
    hi = x.astype(bf16)
    rest = x - hi.astype(f32)
    mid = rest.astype(bf16)
    low = (rest - mid.astype(f32)).astype(bf16)
    return hi, mid, low


def pattern(first, frac):
    cells = lax.broadcasted_iota(i32, (CELLS, first.shape[1]), 0)
    k = (cells - first) & (CELLS - 1)
    dist = (k - (KSUP // 2 - 1)).astype(f32) - frac
    value = jnp.where(k < KSUP, jnp.exp(-0.5 * dist * dist), 0.0).astype(bf16)
    return value, ((first + k) >> 4).astype(f32).astype(bf16)


def dense(value, where, side):
    zero = jnp.zeros_like(value)
    blocks = [jnp.where(where == jnp.bfloat16(b), value, zero) for b in range(side // CELLS)]
    return jnp.concatenate(blocks, axis=0)


def pack_body(tile_row, offset, frac, vis, weight, flag, packed, rank_out, *, devices, per_dev):
    n = tile_row.shape[1]
    t_row = tile_row[...]
    across = jnp.broadcast_to(t_row.astype(f32), (128, n)).T
    parts = []
    for c in range(n // 128):
        part = t_row[:, c * 128 : (c + 1) * 128].astype(f32)
        before = lax.broadcasted_iota(i32, (n, 128), 0)
        before = before < lax.broadcasted_iota(i32, (n, 128), 1) + c * 128
        same = jnp.where((across == part) & before, 1.0, 0.0)
        parts.append(jnp.sum(same, axis=0, keepdims=True))
    rank = jnp.concatenate(parts, axis=1).astype(i32)
    rank_out[...] = rank
    owner = t_row // per_dev
    local = t_row - owner * per_dev
    owners = lax.broadcasted_iota(i32, (devices, n), 0) == owner
    places = MOST * per_dev
    hot = lax.broadcasted_iota(i32, (places, n), 0) == rank * per_dev + local
    hot = hot.astype(f32).astype(bf16)
    rows = [
        offset[0:1, :].astype(f32),
        offset[1:2, :].astype(f32),
        frac[0:1, :],
        frac[1:2, :],
        vis[0:1, :],
        vis[1:2, :],
        weight[...] * flag[...].astype(f32),
    ]
    packed[...] = jnp.zeros(packed.shape, f32)
    for f in range(USED):
        spread = jnp.where(owners, rows[f], 0.0)
        total = jnp.zeros((devices, places), f32)
        for part in split3(spread):
            total = total + lax.dot_general(part, hot, NT_DIMS, preferred_element_type=f32)
        for k in range(MOST):
            at = (k * FIELDS + f) * per_dev
            packed[:, at : at + per_dev] = total[:, k * per_dev : (k + 1) * per_dev]


def predict_body(recv, model, sent, back, fields, *, per_dev):
    side = model.shape[2]
    lanes = back.shape[2]
    l = pl.program_id(0)

    @pl.when(l == 0)
    def _():
        turned = recv[...].T
        span = FIELDS * per_dev
        for k in range(MOST):
            some = turned[k * span : (k + 1) * span, :]
            width = some.shape[1]
            for t in range(per_dev):
                for f in range(FIELDS):
                    at = f * per_dev + t
                    fields[t, f : f + 1, k * width : (k + 1) * width] = some[at : at + 1, :]

    rows = fields[l]
    first = rows[0:2].astype(i32) - (KSUP // 2 - 1)
    ku = dense(*pattern(first[0:1], rows[2:3]), side)
    kv = dense(*pattern(first[1:2], rows[3:4]), side).astype(f32)
    residual = []
    for c in range(2):
        product = lax.dot_general(model[0, c], ku, NN_DIMS, preferred_element_type=f32)
        predicted = jnp.sum(product * kv, axis=0, keepdims=True)
        residual.append(rows[6:7] * (predicted - rows[4 + c : 5 + c]))
    back[0] = jnp.concatenate(residual, axis=0)
    there = rows[0:1] > 0.5
    above = lax.broadcasted_iota(i32, (lanes, lanes), 0) < lax.broadcasted_iota(i32, (lanes, lanes), 1)
    above = above.astype(f32).astype(bf16)
    ones = jnp.broadcast_to(there.astype(f32), (8, lanes)).astype(bf16)
    place = lax.dot_general(ones, above, NN_DIMS, preferred_element_type=f32)[0:1]
    place = jnp.where(there, place, -1.0).astype(i32)
    move = lax.broadcasted_iota(i32, (lanes, lanes), 0) == place
    move = move.astype(f32).astype(bf16)
    all_rows = jnp.concatenate([rows[0:4]] + residual + [jnp.zeros((2, lanes), f32)], axis=0)
    total = jnp.zeros((8, lanes), f32)
    for part in split3(all_rows):
        total = total + lax.dot_general(part, move, NT_DIMS, preferred_element_type=f32)
    sent[0] = total[0:SENT]


def fft_pos(z):
    n = len(z)
    if n == 1:
        return z
    even = fft_pos(z[0::2])
    odd = fft_pos(z[1::2])
    low, high = [], []
    for k in range(n // 2):
        o_re, o_im = odd[k]
        if k == 0:
            t_re, t_im = o_re, o_im
        elif 4 * k == n:
            t_re, t_im = -o_im, o_re
        else:
            c, s = math.cos(2 * math.pi * k / n), math.sin(2 * math.pi * k / n)
            t_re = o_re * c - o_im * s
            t_im = o_re * s + o_im * c
        e_re, e_im = even[k]
        low.append((e_re + t_re, e_im + t_im))
        high.append((e_re - t_re, e_im - t_im))
    return low + high


def image_body(
    counts, tiles, turn_u, rot, turn_v, twist, out,
    merged, kv_all, up_all, grid, turned, stage, sems, *flips,
):
    side = turn_u.shape[1]
    rows2 = turn_u.shape[0]
    rows = rows2 // 2
    lanes = tiles.shape[2]
    width = flips[0].shape[1]
    most = NT * lanes

    def tile_column(tv, carry):
        group = tv // TVG * (NT * TVG) + tv % TVG
        merged[...] = jnp.zeros(merged.shape, f32)
        used = jnp.int32(0)
        for tu in range(NT):
            tile = group + tu * TVG
            base = pl.multiple_of(used // 128 * 128, 128)
            cell = tiles[tile]
            tail = jnp.zeros((SENT, 128), f32)
            moved = pltpu.roll(jnp.concatenate([cell, tail], axis=1), used % 128, axis=1)
            at = (slice(0, SENT), pl.ds(base, lanes + 128))
            merged[at] = merged[at] + moved
            at = (slice(SENT, SENT + 1), pl.ds(base, lanes + 128))
            mark = jnp.full((1, lanes + 128), float(tu), f32)
            here = lax.broadcasted_iota(i32, mark.shape, 1) >= used % 128
            merged[at] = jnp.where(here, mark, merged[at])
            used = used + counts[tile]
        chunks = jnp.maximum(1, (used + CHUNK - 1) // CHUNK)

        def chunk(i, c):
            at = pl.multiple_of(i * CHUNK, CHUNK)
            m = merged[:, pl.ds(at, CHUNK)]
            first = m[0:2].astype(i32) - (KSUP // 2 - 1)
            ku = dense(*pattern(first[0:1], m[2:3]), side)
            kv_all[:, pl.ds(at, CHUNK)] = dense(*pattern(first[1:2], m[3:4]), side)
            v = lax.dot_general(turn_u[...], ku, NN_DIMS, preferred_element_type=f32)
            r_re = m[4:5] * (1.0 / NPIX)
            r_im = m[5:6] * (1.0 / NPIX)
            which = lax.broadcasted_iota(i32, (NT, CHUNK), 0).astype(f32) == m[6:7]
            which = which.astype(f32).astype(bf16)
            turn = jnp.zeros((2 * NT, CHUNK), f32)
            for j in range(3):
                turn = turn + lax.dot_general(rot[j], which, NN_DIMS, preferred_element_type=f32)
            cos_t, sin_t = turn[:NT], turn[NT:]
            c_re = (r_re * cos_t - r_im * sin_t)[None]
            c_im = (r_re * sin_t + r_im * cos_t)[None]
            v_re = v[:rows].reshape(rows // NT, NT, CHUNK)
            v_im = v[rows:].reshape(rows // NT, NT, CHUNK)
            u_re = (c_re * v_re - c_im * v_im).reshape(rows, CHUNK)
            u_im = (c_re * v_im + c_im * v_re).reshape(rows, CHUNK)
            up_all[0:rows, pl.ds(at, CHUNK)] = u_re.astype(bf16)
            up_all[rows:rows2, pl.ds(at, CHUNK)] = u_im.astype(bf16)
            return c

        lax.fori_loop(0, chunks, chunk, 0)

        if most // CHUNK <= 8:
            for n in range(1, most // CHUNK + 1):

                @pl.when(chunks == n)
                def _():
                    ft = lax.dot_general(
                        kv_all[:, 0 : n * CHUNK],
                        up_all[:, 0 : n * CHUNK],
                        NT_DIMS,
                        preferred_element_type=f32,
                    )
                    grid[tv] = ft.astype(bf16)

        else:

            def add(i, ft):
                at = pl.multiple_of(i * CHUNK, CHUNK)
                return ft + lax.dot_general(
                    kv_all[:, pl.ds(at, CHUNK)],
                    up_all[:, pl.ds(at, CHUNK)],
                    NT_DIMS,
                    preferred_element_type=f32,
                )

            ft = lax.fori_loop(0, chunks, add, jnp.zeros((side, rows2), f32))
            grid[tv] = ft.astype(bf16)
        return carry

    lax.fori_loop(0, NT, tile_column, 0)

    def stripe(j, carry):
        r0 = pl.multiple_of(j * 16, 16)
        tc = twist[0, pl.ds(r0, 16), :]
        ts = twist[1, pl.ds(r0, 16), :]
        for h in range(rows // width):
            c0 = h * width
            z = [
                (
                    grid[t, pl.ds(r0, 16), c0 : c0 + width].astype(f32),
                    grid[t, pl.ds(r0, 16), rows + c0 : rows + c0 + width].astype(f32),
                )
                for t in range(NT)
            ]
            x = fft_pos(z)
            for n0 in range(NT):
                re, im = x[n0]
                if n0 > 0:
                    c = tc[:, n0 : n0 + 1]
                    s = ts[:, n0 : n0 + 1]
                    re, im = re * c - im * s, re * s + im * c
                turned[n0, pl.ds(r0, 16), c0 : c0 + width] = re.astype(bf16)
                turned[n0, pl.ds(r0 + side, 16), c0 : c0 + width] = im.astype(bf16)
        return carry

    lax.fori_loop(0, side // 16, stripe, 0)

    for n0 in range(NT):
        x = lax.dot_general(turn_v[...], turned[n0], NN_DIMS, preferred_element_type=f32)
        for h in range(rows // width):
            flips[h][pl.ds(n0, side, stride=NT), :] = x[:, h * width : (h + 1) * width]

    pieces = sems.shape[0]
    wide = NPIX // pieces
    copies = []
    for i in range(pieces):
        for h in range(rows // width):
            stage[h * width : (h + 1) * width, i * wide : (i + 1) * wide] = (
                flips[h][i * wide : (i + 1) * wide, :].T
            )
        copy = pltpu.make_async_copy(
            stage.at[:, pl.ds(i * wide, wide)], out.at[:, pl.ds(i * wide, wide)], sems.at[i]
        )
        copy.start()
        copies.append(copy)
    for copy in copies:
        copy.wait()


def own_body(res, tile_row, rank, out, *, per_dev):
    devices = res.shape[0]
    n = tile_row.shape[1]
    t_row = tile_row[...]
    owner = t_row // per_dev
    local = t_row - owner * per_dev
    hot = lax.broadcasted_iota(i32, (devices, n), 0) == owner
    hot = hot.astype(f32).astype(bf16)
    places = MOST * per_dev
    mine = lax.broadcasted_iota(i32, (places, n), 0) == rank[...] * per_dev + local
    turned = res[...].T
    total = jnp.zeros((2 * places, n), f32)
    for part in split3(turned):
        total = total + lax.dot_general(part, hot, NN_DIMS, preferred_element_type=f32)
    for c in range(2):
        some = total[c * places : (c + 1) * places]
        out[c : c + 1, :] = jnp.sum(jnp.where(mine, some, 0.0), axis=0, keepdims=True)


def cos_sin(product, period):
    angle = (2.0 * math.pi / period) * (product % period).astype(f32)
    return jnp.cos(angle), jnp.sin(angle)


def exchange(x):
    return lax.all_to_all(x, AXES, split_axis=0, concat_axis=0, tiled=True)


def on_device(model_grid, vis_values, weights, flags, uv_frac, cell_offset, tile_index):
    devices = lax.axis_size("blen") * lax.axis_size("tm")
    me = lax.axis_index("blen") * lax.axis_size("tm") + lax.axis_index("tm")
    per_dev = model_grid.shape[0]
    side = model_grid.shape[2]
    n = weights.shape[0]
    ntiles = per_dev * devices
    lanes = devices * MOST
    rows = NPIX // devices
    call = pl.pallas_call
    shape = jax.ShapeDtypeStruct

    tile_row = tile_index.reshape(1, n)
    width = MOST * FIELDS * per_dev
    packed, rank = call(
        lambda *refs: pack_body(*refs, devices=devices, per_dev=per_dev),
        out_shape=(shape((devices, width), f32), shape((1, n), i32)),
        name="pack",
    )(tile_row, cell_offset, uv_frac, vis_values, weights.reshape(1, n), flags.reshape(1, n))
    recv = exchange(packed)
    sent, back = call(
        lambda *refs: predict_body(*refs, per_dev=per_dev),
        grid=(per_dev,),
        in_specs=[
            pl.BlockSpec((devices, width), lambda l: (0, 0)),
            pl.BlockSpec((1, 2, side, side), lambda l: (l, 0, 0, 0)),
        ],
        out_specs=(
            pl.BlockSpec((1, SENT, lanes), lambda l: (l, 0, 0)),
            pl.BlockSpec((1, 2, lanes), lambda l: (l, 0, 0)),
        ),
        out_shape=(shape((per_dev, SENT, lanes), f32), shape((per_dev, 2, lanes), f32)),
        scratch_shapes=[pltpu.VMEM((per_dev, FIELDS, lanes), f32)],
        compiler_params=params(32),
        name="predict",
    )(recv, model_grid)
    tiles = exchange(jnp.broadcast_to(sent[None], (devices,) + sent.shape))
    tiles = tiles.reshape(ntiles, SENT, lanes)
    counts = jnp.sum((tiles[:, 0, :] > 0.5).astype(i32), axis=1)
    back, counts = lax.optimization_barrier((back, counts))
    returned = back.reshape(per_dev, 2, MOST, devices).transpose(3, 1, 2, 0)
    returned = exchange(returned.reshape(devices, 2 * MOST * per_dev))

    image_rows = me * rows + jnp.arange(rows, dtype=i32)
    cells = jnp.arange(side, dtype=i32)
    small = jnp.arange(NT, dtype=i32)
    turn_u = jnp.concatenate(cos_sin(image_rows[:, None] * cells[None, :], NPIX)).astype(bf16)
    rot = jnp.stack(split3(jnp.concatenate(cos_sin(small[:, None] * small[None, :], NT))))
    cos_v, sin_v = cos_sin(cells[:, None] * cells[None, :], side)
    turn_v = jnp.concatenate([cos_v, -sin_v], axis=1).astype(bf16)
    twist = jnp.stack(cos_sin(cells[:, None] * small[None, :], NPIX))
    thin = min(128, rows)
    vmem = pl.BlockSpec(memory_space=pltpu.VMEM)
    gradient = call(
        image_body,
        in_specs=[pl.BlockSpec(memory_space=pltpu.SMEM)] + [vmem] * 5,
        out_specs=pl.BlockSpec(memory_space=pl.ANY),
        out_shape=shape((rows, NPIX), f32),
        scratch_shapes=[
            pltpu.VMEM((8, NT * lanes + 128), f32),
            pltpu.VMEM((side, NT * lanes), bf16),
            pltpu.VMEM((2 * rows, NT * lanes), bf16),
            pltpu.VMEM((NT, side, 2 * rows), bf16),
            pltpu.VMEM((NT, 2 * side, rows), bf16),
            pltpu.VMEM((rows, NPIX), f32),
            pltpu.SemaphoreType.DMA((8,)),
        ]
        + [pltpu.VMEM((NPIX, thin), f32)] * (rows // thin),
        compiler_params=params(56),
        name="image",
    )(counts, tiles, turn_u, rot, turn_v, twist)
    weighted_residual = call(
        lambda *refs: own_body(*refs, per_dev=per_dev),
        out_shape=shape((2, n), f32),
        name="own",
    )(returned, tile_row, rank)
    return (gradient, weighted_residual)


def solution(mesh):
    in_specs = (
        P(AXES, None, None, None),
        P(None, AXES),
        P(AXES),
        P(AXES),
        P(None, AXES),
        P(None, AXES),
        P(AXES, None),
    )
    out_specs = (P(AXES, None), P(None, AXES))
    return jax.shard_map(
        on_device, mesh=mesh, in_specs=in_specs, out_specs=out_specs, check_vma=False
    )
```

```python
import math

import jax
import jax.numpy as jnp
from jax import lax
from jax.experimental import pallas as pl
from jax.experimental.pallas import tpu as pltpu
from jax.sharding import PartitionSpec as P

NPIX = 8192
KSUP = 8
NT = 16
TVG = 4
MOST = 4
FIELDS = 8
USED = 7
SENT = 6
CELLS = 16
CHUNK = 256

AXES = ("blen", "tm")
f32 = jnp.float32
bf16 = jnp.bfloat16
i32 = jnp.int32
NT_DIMS = (((1,), (1,)), ((), ()))
NN_DIMS = (((1,), (0,)), ((), ()))
MIB = 1 << 20


def params(mib):
    return pltpu.CompilerParams(vmem_limit_bytes=mib * MIB)


def split3(x):
    hi = x.astype(bf16)
    rest = x - hi.astype(f32)
    mid = rest.astype(bf16)
    low = (rest - mid.astype(f32)).astype(bf16)
    return hi, mid, low


def pattern(first, frac):
    cells = lax.broadcasted_iota(i32, (CELLS, first.shape[1]), 0)
    k = (cells - first) & (CELLS - 1)
    dist = (k - (KSUP // 2 - 1)).astype(f32) - frac
    value = jnp.where(k < KSUP, jnp.exp(-0.5 * dist * dist), 0.0).astype(bf16)
    return value, ((first + k) >> 4).astype(f32).astype(bf16)


def dense(value, where, side):
    zero = jnp.zeros_like(value)
    blocks = [jnp.where(where == jnp.bfloat16(b), value, zero) for b in range(side // CELLS)]
    return jnp.concatenate(blocks, axis=0)


def pack_body(tile_row, offset, frac, vis, weight, flag, packed, rank_out, *, devices, per_dev):
    n = tile_row.shape[1]
    t_row = tile_row[...]
    across = jnp.broadcast_to(t_row.astype(f32), (128, n)).T
    parts = []
    for c in range(n // 128):
        part = t_row[:, c * 128 : (c + 1) * 128].astype(f32)
        before = lax.broadcasted_iota(i32, (n, 128), 0)
        before = before < lax.broadcasted_iota(i32, (n, 128), 1) + c * 128
        same = jnp.where((across == part) & before, 1.0, 0.0)
        parts.append(jnp.sum(same, axis=0, keepdims=True))
    rank = jnp.concatenate(parts, axis=1).astype(i32)
    rank_out[...] = rank
    owner = t_row // per_dev
    local = t_row - owner * per_dev
    owners = lax.broadcasted_iota(i32, (devices, n), 0) == owner
    places = MOST * per_dev
    hot = lax.broadcasted_iota(i32, (places, n), 0) == rank * per_dev + local
    hot = hot.astype(f32).astype(bf16)
    rows = [
        offset[0:1, :].astype(f32),
        offset[1:2, :].astype(f32),
        frac[0:1, :],
        frac[1:2, :],
        vis[0:1, :],
        vis[1:2, :],
        weight[...] * flag[...].astype(f32),
    ]
    packed[...] = jnp.zeros(packed.shape, f32)
    for f in range(USED):
        spread = jnp.where(owners, rows[f], 0.0)
        total = jnp.zeros((devices, places), f32)
        for part in split3(spread):
            total = total + lax.dot_general(part, hot, NT_DIMS, preferred_element_type=f32)
        for k in range(MOST):
            at = (k * FIELDS + f) * per_dev
            packed[:, at : at + per_dev] = total[:, k * per_dev : (k + 1) * per_dev]


def predict_body(recv, model, sent, back, fields, *, per_dev):
    side = model.shape[2]
    lanes = back.shape[2]
    l = pl.program_id(0)

    @pl.when(l == 0)
    def _():
        turned = recv[...].T
        span = FIELDS * per_dev
        for k in range(MOST):
            some = turned[k * span : (k + 1) * span, :]
            width = some.shape[1]
            for t in range(per_dev):
                for f in range(FIELDS):
                    at = f * per_dev + t
                    fields[t, f : f + 1, k * width : (k + 1) * width] = some[at : at + 1, :]

    rows = fields[l]
    first = rows[0:2].astype(i32) - (KSUP // 2 - 1)
    ku = dense(*pattern(first[0:1], rows[2:3]), side)
    kv = dense(*pattern(first[1:2], rows[3:4]), side).astype(f32)
    for c in range(2):
        product = lax.dot_general(model[0, c], ku, NN_DIMS, preferred_element_type=f32)
        predicted = jnp.sum(product * kv, axis=0, keepdims=True)
        residual = rows[6:7] * (predicted - rows[4 + c : 5 + c])
        fields[l, 4 + c : 5 + c, :] = residual
        back[l, c : c + 1, :] = residual

    @pl.when(l == per_dev - 1)
    def _():
        above = lax.broadcasted_iota(i32, (lanes, lanes), 0)
        above = above < lax.broadcasted_iota(i32, (lanes, lanes), 1)
        above = above.astype(f32).astype(bf16)
        there = jnp.concatenate([fields[t, 0:1, :] for t in range(per_dev)], axis=0) > 0.5
        place = lax.dot_general(
            there.astype(f32).astype(bf16), above, NN_DIMS, preferred_element_type=f32
        )
        place = jnp.where(there, place, -1.0).astype(i32)
        for t in range(per_dev):
            move = lax.broadcasted_iota(i32, (lanes, lanes), 0) == place[t : t + 1]
            move = move.astype(f32).astype(bf16)
            parts = jnp.concatenate(split3(fields[t]), axis=0)
            total = lax.dot_general(parts, move, NT_DIMS, preferred_element_type=f32)
            total = total[0:8] + total[8:16] + total[16:24]
            sent[t] = total[0:SENT]


def fft_pos(z):
    n = len(z)
    if n == 1:
        return z
    even = fft_pos(z[0::2])
    odd = fft_pos(z[1::2])
    low, high = [], []
    for k in range(n // 2):
        o_re, o_im = odd[k]
        if k == 0:
            t_re, t_im = o_re, o_im
        elif 4 * k == n:
            t_re, t_im = -o_im, o_re
        else:
            c, s = math.cos(2 * math.pi * k / n), math.sin(2 * math.pi * k / n)
            t_re = o_re * c - o_im * s
            t_im = o_re * s + o_im * c
        e_re, e_im = even[k]
        low.append((e_re + t_re, e_im + t_im))
        high.append((e_re - t_re, e_im - t_im))
    return low + high


def image_body(
    tiles, turn_u, rot, turn_v, twist, out,
    merged, kv_all, up_all, grid, turned, stage, sems, tally, counts, *flips,
):
    side = turn_u.shape[1]
    rows2 = turn_u.shape[0]
    rows = rows2 // 2
    lanes = tiles.shape[2]
    width = flips[0].shape[1]
    most = NT * lanes // CHUNK

    there = jnp.where(tiles[:, 0, :] > 0.5, 1.0, 0.0).astype(bf16)
    total = lax.dot_general(
        jnp.ones((8, lanes), bf16), there, NT_DIMS, preferred_element_type=f32
    )
    tally[...] = total.astype(i32)
    count_copy = pltpu.make_async_copy(tally, counts, sems.at[0])
    count_copy.start()
    count_copy.wait()

    def chunk(at):
        m = merged[:, pl.ds(at, CHUNK)]
        first = m[0:2].astype(i32) - (KSUP // 2 - 1)
        ku = dense(*pattern(first[0:1], m[2:3]), side)
        kv_all[:, pl.ds(at, CHUNK)] = dense(*pattern(first[1:2], m[3:4]), side)
        v = lax.dot_general(turn_u[...], ku, NN_DIMS, preferred_element_type=f32)
        r_re = m[4:5] * (1.0 / NPIX)
        r_im = m[5:6] * (1.0 / NPIX)
        which = lax.broadcasted_iota(i32, (NT, CHUNK), 0).astype(f32) == m[6:7]
        which = which.astype(f32).astype(bf16)
        which = jnp.concatenate([which] * 3, axis=0)
        turn = lax.dot_general(rot[...], which, NN_DIMS, preferred_element_type=f32)
        cos_t, sin_t = turn[:NT], turn[NT:]
        c_re = (r_re * cos_t - r_im * sin_t)[None]
        c_im = (r_re * sin_t + r_im * cos_t)[None]
        v_re = v[:rows].reshape(rows // NT, NT, CHUNK)
        v_im = v[rows:].reshape(rows // NT, NT, CHUNK)
        u_re = (c_re * v_re - c_im * v_im).reshape(rows, CHUNK)
        u_im = (c_re * v_im + c_im * v_re).reshape(rows, CHUNK)
        up_all[0:rows, pl.ds(at, CHUNK)] = u_re.astype(bf16)
        up_all[rows:rows2, pl.ds(at, CHUNK)] = u_im.astype(bf16)

    def product(at, size):
        return lax.dot_general(
            kv_all[:, pl.ds(at, size)],
            up_all[:, pl.ds(at, size)],
            NT_DIMS,
            preferred_element_type=f32,
        )

    def tile_column(tv, carry):
        group = tv // TVG * (NT * TVG) + tv % TVG
        merged[...] = jnp.zeros(merged.shape, f32)
        used = jnp.int32(0)
        for tu in range(NT):
            tile = group + tu * TVG
            cell = tiles[tile]
            mark = jnp.where(cell[0:1] > 0.5, float(tu), 0.0)
            cell = jnp.concatenate([cell, mark, jnp.zeros((1, lanes), f32)], axis=0)
            cell = jnp.concatenate([cell, jnp.zeros((8, 128), f32)], axis=1)
            at = pl.ds(pl.multiple_of(used // 128 * 128, 128), lanes + 128)
            merged[:, at] = merged[:, at] + pltpu.roll(cell, used % 128, axis=1)
            used = used + counts[0, tile]
        chunks = (used + CHUNK - 1) // CHUNK

        if most == 8:
            low = -1
            for n in (2, 4, 5, 6, 8):

                @pl.when((chunks > low) & (chunks <= n))
                def _():
                    for i in range(n):
                        chunk(i * CHUNK)
                    grid[tv] = product(0, n * CHUNK).astype(bf16)

                low = n
        else:

            def make(i, c):
                chunk(pl.multiple_of(i * CHUNK, CHUNK))
                return c

            def add(i, ft):
                return ft + product(pl.multiple_of(i * CHUNK, CHUNK), CHUNK)

            lax.fori_loop(0, chunks, make, 0)
            ft = lax.fori_loop(0, chunks, add, jnp.zeros((side, rows2), f32))
            grid[tv] = ft.astype(bf16)
        return carry

    lax.fori_loop(0, NT, tile_column, 0)

    def stripe(j, carry):
        r0 = pl.multiple_of(j * 16, 16)
        tc = twist[0, pl.ds(r0, 16), :]
        ts = twist[1, pl.ds(r0, 16), :]
        for h in range(rows // width):
            c0 = h * width
            z = [
                (
                    grid[t, pl.ds(r0, 16), c0 : c0 + width].astype(f32),
                    grid[t, pl.ds(r0, 16), rows + c0 : rows + c0 + width].astype(f32),
                )
                for t in range(NT)
            ]
            x = fft_pos(z)
            for n0 in range(NT):
                re, im = x[n0]
                if n0 > 0:
                    c = tc[:, n0 : n0 + 1]
                    s = ts[:, n0 : n0 + 1]
                    re, im = re * c - im * s, re * s + im * c
                turned[n0, pl.ds(r0, 16), c0 : c0 + width] = re.astype(bf16)
                turned[n0, pl.ds(r0 + side, 16), c0 : c0 + width] = im.astype(bf16)
        return carry

    lax.fori_loop(0, side // 16, stripe, 0)

    for n0 in range(NT):
        x = lax.dot_general(turn_v[...], turned[n0], NN_DIMS, preferred_element_type=f32)
        for h in range(rows // width):
            flips[h][pl.ds(n0, side, stride=NT), :] = x[:, h * width : (h + 1) * width]

    pieces = sems.shape[0]
    wide = NPIX // pieces
    copies = []
    for i in range(pieces):
        for h in range(rows // width):
            stage[h * width : (h + 1) * width, i * wide : (i + 1) * wide] = (
                flips[h][i * wide : (i + 1) * wide, :].T
            )
        copy = pltpu.make_async_copy(
            stage.at[:, pl.ds(i * wide, wide)], out.at[:, pl.ds(i * wide, wide)], sems.at[i]
        )
        copy.start()
        copies.append(copy)
    for copy in copies:
        copy.wait()


def own_body(res, tile_row, rank, out, *, per_dev):
    devices = res.shape[0]
    n = tile_row.shape[1]
    t_row = tile_row[...]
    owner = t_row // per_dev
    local = t_row - owner * per_dev
    hot = lax.broadcasted_iota(i32, (devices, n), 0) == owner
    hot = hot.astype(f32).astype(bf16)
    places = MOST * per_dev
    mine = lax.broadcasted_iota(i32, (places, n), 0) == rank[...] * per_dev + local
    turned = res[...].T
    total = jnp.zeros((2 * places, n), f32)
    for part in split3(turned):
        total = total + lax.dot_general(part, hot, NN_DIMS, preferred_element_type=f32)
    for c in range(2):
        some = total[c * places : (c + 1) * places]
        out[c : c + 1, :] = jnp.sum(jnp.where(mine, some, 0.0), axis=0, keepdims=True)


def cos_sin(product, period):
    angle = (2.0 * math.pi / period) * (product % period).astype(f32)
    return jnp.cos(angle), jnp.sin(angle)


def exchange(x):
    return lax.all_to_all(x, AXES, split_axis=0, concat_axis=0, tiled=True)


def on_device(model_grid, vis_values, weights, flags, uv_frac, cell_offset, tile_index):
    devices = lax.axis_size("blen") * lax.axis_size("tm")
    me = lax.axis_index("blen") * lax.axis_size("tm") + lax.axis_index("tm")
    per_dev = model_grid.shape[0]
    side = model_grid.shape[2]
    n = weights.shape[0]
    ntiles = per_dev * devices
    lanes = devices * MOST
    rows = NPIX // devices
    call = pl.pallas_call
    shape = jax.ShapeDtypeStruct

    tile_row = tile_index.reshape(1, n)
    width = MOST * FIELDS * per_dev
    packed, rank = call(
        lambda *refs: pack_body(*refs, devices=devices, per_dev=per_dev),
        out_shape=(shape((devices, width), f32), shape((1, n), i32)),
        name="pack",
    )(tile_row, cell_offset, uv_frac, vis_values, weights.reshape(1, n), flags.reshape(1, n))
    recv = exchange(packed)
    sent, back = call(
        lambda *refs: predict_body(*refs, per_dev=per_dev),
        grid=(per_dev,),
        in_specs=[
            pl.BlockSpec((devices, width), lambda l: (0, 0)),
            pl.BlockSpec((1, 2, side, side), lambda l: (l, 0, 0, 0)),
        ],
        out_specs=(
            pl.BlockSpec((per_dev, SENT, lanes), lambda l: (0, 0, 0)),
            pl.BlockSpec((per_dev, 2, lanes), lambda l: (0, 0, 0)),
        ),
        out_shape=(shape((per_dev, SENT, lanes), f32), shape((per_dev, 2, lanes), f32)),
        scratch_shapes=[pltpu.VMEM((per_dev, FIELDS, lanes), f32)],
        compiler_params=params(32),
        name="predict",
    )(recv, pltpu.with_memory_space_constraint(model_grid, pltpu.HBM))
    tiles = exchange(jnp.broadcast_to(sent[None], (devices,) + sent.shape))
    tiles = tiles.reshape(ntiles, SENT, lanes)
    back, tiles = lax.optimization_barrier((back, tiles))
    returned = back.reshape(per_dev, 2, MOST, devices).transpose(3, 1, 2, 0)
    returned = exchange(returned.reshape(devices, 2 * MOST * per_dev))

    image_rows = me * rows + jnp.arange(rows, dtype=i32)
    cells = jnp.arange(side, dtype=i32)
    small = jnp.arange(NT, dtype=i32)
    turn_u = jnp.concatenate(cos_sin(image_rows[:, None] * cells[None, :], NPIX)).astype(bf16)
    rot = cos_sin(small[:, None] * small[None, :], NT)
    rot = jnp.concatenate(split3(jnp.concatenate(rot)), axis=1)
    cos_v, sin_v = cos_sin(cells[:, None] * cells[None, :], side)
    turn_v = jnp.concatenate([cos_v, -sin_v], axis=1).astype(bf16)
    twist = jnp.stack(cos_sin(cells[:, None] * small[None, :], NPIX))
    thin = min(128, rows)
    vmem = pl.BlockSpec(memory_space=pltpu.VMEM)
    gradient = call(
        image_body,
        in_specs=[vmem] * 5,
        out_specs=pl.BlockSpec(memory_space=pl.ANY),
        out_shape=shape((rows, NPIX), f32),
        scratch_shapes=[
            pltpu.VMEM((8, NT * lanes + 128), f32),
            pltpu.VMEM((side, NT * lanes), bf16),
            pltpu.VMEM((2 * rows, NT * lanes), bf16),
            pltpu.VMEM((NT, side, 2 * rows), bf16),
            pltpu.VMEM((NT, 2 * side, rows), bf16),
            pltpu.VMEM((rows, NPIX), f32),
            pltpu.SemaphoreType.DMA((8,)),
            pltpu.VMEM((8, ntiles), i32),
            pltpu.SMEM((8, ntiles), i32),
        ]
        + [pltpu.VMEM((NPIX, thin), f32)] * (rows // thin),
        compiler_params=params(56),
        name="image",
    )(tiles, turn_u, rot, turn_v, twist)
    weighted_residual = call(
        lambda *refs: own_body(*refs, per_dev=per_dev),
        out_shape=shape((2, n), f32),
        name="own",
    )(returned, tile_row, rank)
    return (gradient, weighted_residual)


def solution(mesh):
    in_specs = (
        P(AXES, None, None, None),
        P(None, AXES),
        P(AXES),
        P(AXES),
        P(None, AXES),
        P(None, AXES),
        P(AXES, None),
    )
    out_specs = (P(AXES, None), P(None, AXES))
    return jax.shard_map(
        on_device, mesh=mesh, in_specs=in_specs, out_specs=out_specs, check_vma=False
    )
```

```python
import math

import jax
import jax.numpy as jnp
from jax import lax
from jax.experimental import pallas as pl
from jax.experimental.pallas import tpu as pltpu
from jax.sharding import PartitionSpec as P

NPIX = 8192
KSUP = 8
NT = 16
TVG = 4
MOST = 4
FIELDS = 8
USED = 7
SENT = 6
CELLS = 16
CHUNK = 256

AXES = ("blen", "tm")
f32 = jnp.float32
bf16 = jnp.bfloat16
i32 = jnp.int32
NT_DIMS = (((1,), (1,)), ((), ()))
NN_DIMS = (((1,), (0,)), ((), ()))
MIB = 1 << 20


def params(mib):
    return pltpu.CompilerParams(vmem_limit_bytes=mib * MIB)


def split3(x):
    hi = x.astype(bf16)
    rest = x - hi.astype(f32)
    mid = rest.astype(bf16)
    low = (rest - mid.astype(f32)).astype(bf16)
    return hi, mid, low


def pattern(first, frac):
    cells = lax.broadcasted_iota(i32, (CELLS, first.shape[1]), 0)
    k = (cells - first) & (CELLS - 1)
    dist = (k - (KSUP // 2 - 1)).astype(f32) - frac
    value = jnp.where(k < KSUP, jnp.exp(-0.5 * dist * dist), 0.0).astype(bf16)
    return value, ((first + k) >> 4).astype(f32).astype(bf16)


def dense(value, where, side):
    zero = jnp.zeros_like(value)
    blocks = [jnp.where(where == jnp.bfloat16(b), value, zero) for b in range(side // CELLS)]
    return jnp.concatenate(blocks, axis=0)


def pack_body(tile_row, offset, frac, vis, weight, flag, packed, rank_out, *, devices, per_dev):
    n = tile_row.shape[1]
    t_row = tile_row[...]
    across = jnp.broadcast_to(t_row.astype(f32), (128, n)).T
    parts = []
    for c in range(n // 128):
        part = t_row[:, c * 128 : (c + 1) * 128].astype(f32)
        before = lax.broadcasted_iota(i32, (n, 128), 0)
        before = before < lax.broadcasted_iota(i32, (n, 128), 1) + c * 128
        same = jnp.where((across == part) & before, 1.0, 0.0)
        parts.append(jnp.sum(same, axis=0, keepdims=True))
    rank = jnp.concatenate(parts, axis=1).astype(i32)
    rank_out[...] = rank
    owner = t_row // per_dev
    local = t_row - owner * per_dev
    owners = lax.broadcasted_iota(i32, (devices, n), 0) == owner
    places = MOST * per_dev
    hot = lax.broadcasted_iota(i32, (places, n), 0) == rank * per_dev + local
    hot = hot.astype(f32).astype(bf16)
    rows = [
        offset[0:1, :].astype(f32),
        offset[1:2, :].astype(f32),
        frac[0:1, :],
        frac[1:2, :],
        vis[0:1, :],
        vis[1:2, :],
        weight[...] * flag[...].astype(f32),
    ]
    packed[...] = jnp.zeros(packed.shape, f32)
    for f in range(USED):
        spread = jnp.where(owners, rows[f], 0.0)
        total = jnp.zeros((devices, places), f32)
        for part in split3(spread):
            total = total + lax.dot_general(part, hot, NT_DIMS, preferred_element_type=f32)
        for k in range(MOST):
            at = (k * FIELDS + f) * per_dev
            packed[:, at : at + per_dev] = total[:, k * per_dev : (k + 1) * per_dev]


def predict_body(recv, model, sent, back, fields, *, per_dev):
    group = model.shape[0]
    side = model.shape[2]
    lanes = sent.shape[1]
    devices = recv.shape[0]
    step = pl.program_id(0)

    @pl.when(step == 0)
    def _():
        turned = recv[...].T
        span = FIELDS * per_dev
        for k in range(MOST):
            some = turned[k * span : (k + 1) * span, :]
            for t in range(per_dev):
                for f in range(FIELDS):
                    at = f * per_dev + t
                    fields[t, f : f + 1, k * devices : (k + 1) * devices] = some[at : at + 1, :]

    for i in range(group):
        l = step * group + i
        rows = fields[l]
        first = rows[0:2].astype(i32) - (KSUP // 2 - 1)
        ku = dense(*pattern(first[0:1], rows[2:3]), side)
        kv = dense(*pattern(first[1:2], rows[3:4]), side).astype(f32)
        for c in range(2):
            product = lax.dot_general(model[i, c], ku, NN_DIMS, preferred_element_type=f32)
            predicted = jnp.sum(product * kv, axis=0, keepdims=True)
            fields[l, 4 + c : 5 + c, :] = rows[6:7] * (predicted - rows[4 + c : 5 + c])

    @pl.when(step == per_dev // group - 1)
    def _():
        above = lax.broadcasted_iota(i32, (lanes, lanes), 0)
        above = above < lax.broadcasted_iota(i32, (lanes, lanes), 1)
        above = above.astype(f32).astype(bf16)
        there = jnp.concatenate([fields[t, 0:1, :] for t in range(per_dev)], axis=0) > 0.5
        place = lax.dot_general(
            there.astype(f32).astype(bf16), above, NN_DIMS, preferred_element_type=f32
        )
        place = jnp.where(there, place, -1.0).astype(i32)
        for t in range(per_dev):
            move = lax.broadcasted_iota(i32, (lanes, lanes), 0) == place[t : t + 1]
            move = move.astype(f32).astype(bf16)
            parts = jnp.concatenate(split3(fields[t]), axis=0)
            total = lax.dot_general(parts, move, NT_DIMS, preferred_element_type=f32)
            total = total[0:8] + total[8:16] + total[16:24]
            sent[t * SENT : (t + 1) * SENT, :] = total[0:SENT]
        mine = [fields[t, 4 + c : 5 + c, :] for c in range(2) for t in range(per_dev)]
        turned = jnp.concatenate(mine, axis=0).T
        back[...] = jnp.zeros(back.shape, f32)
        wide = 2 * per_dev
        for k in range(MOST):
            back[:, k * wide : (k + 1) * wide] = turned[k * devices : (k + 1) * devices, :]


def fft_pos(z):
    n = len(z)
    if n == 1:
        return z
    even = fft_pos(z[0::2])
    odd = fft_pos(z[1::2])
    low, high = [], []
    for k in range(n // 2):
        o_re, o_im = odd[k]
        if k == 0:
            t_re, t_im = o_re, o_im
        elif 4 * k == n:
            t_re, t_im = -o_im, o_re
        else:
            c, s = math.cos(2 * math.pi * k / n), math.sin(2 * math.pi * k / n)
            t_re = o_re * c - o_im * s
            t_im = o_re * s + o_im * c
        e_re, e_im = even[k]
        low.append((e_re + t_re, e_im + t_im))
        high.append((e_re - t_re, e_im - t_im))
    return low + high


def image_body(
    recv, tile_row, rank, turn_u, rot, turn_v, twist, out, own,
    tiles, merged, kv_all, up_all, grid, turned, stage, sems, tally, counts, *flips,
):
    side = turn_u.shape[1]
    rows2 = turn_u.shape[0]
    rows = rows2 // 2
    devices = recv.shape[0]
    lanes = recv.shape[2]
    per_dev = recv.shape[1] // SENT
    width = flips[0].shape[1]
    most = NT * lanes // CHUNK

    there = []
    for l in range(per_dev):
        some = recv[:, l * SENT : (l + 1) * SENT, :]
        filled = some[:, 0:1, :] > 0.5
        tile = lax.broadcasted_iota(i32, filled.shape, 0) * per_dev + l
        mark = jnp.where(filled, (tile // TVG % NT).astype(f32), 0.0)
        tiles[:, l] = jnp.concatenate([some, mark, jnp.zeros_like(mark)], axis=1)
        there.append(jnp.where(filled[:, 0], 1.0, 0.0).astype(bf16))
    total = lax.dot_general(
        jnp.ones((8, lanes), bf16),
        jnp.concatenate(there, axis=0),
        NT_DIMS,
        preferred_element_type=f32,
    )
    tally[...] = total.astype(i32)
    count_copy = pltpu.make_async_copy(tally, counts, sems.at[0])
    count_copy.start()

    n = tile_row.shape[1]
    t_row = tile_row[...]
    owner = t_row // per_dev
    local = t_row - owner * per_dev
    hot = lax.broadcasted_iota(i32, (devices, n), 0) == owner
    hot = hot.astype(f32).astype(bf16)
    mine = jnp.concatenate(split3(recv[:, per_dev * SENT, :].T), axis=0)
    total = lax.dot_general(mine, hot, NN_DIMS, preferred_element_type=f32)
    total = total[0:lanes] + total[lanes : 2 * lanes] + total[2 * lanes : 3 * lanes]
    places = lax.broadcasted_iota(i32, (lanes, n), 0)
    for c in range(2):
        picked = places == (rank[...] * 2 + c) * per_dev + local
        own[c : c + 1, :] = jnp.sum(jnp.where(picked, total, 0.0), axis=0, keepdims=True)
    count_copy.wait()

    def chunk(at):
        m = merged[:, pl.ds(at, CHUNK)]
        first = m[0:2].astype(i32) - (KSUP // 2 - 1)
        ku = dense(*pattern(first[0:1], m[2:3]), side)
        kv_all[:, pl.ds(at, CHUNK)] = dense(*pattern(first[1:2], m[3:4]), side)
        v = lax.dot_general(turn_u[...], ku, NN_DIMS, preferred_element_type=f32)
        r_re = m[4:5] * (1.0 / NPIX)
        r_im = m[5:6] * (1.0 / NPIX)
        which = lax.broadcasted_iota(i32, (NT, CHUNK), 0).astype(f32) == m[6:7]
        which = which.astype(f32).astype(bf16)
        which = jnp.concatenate([which] * 3, axis=0)
        turn = lax.dot_general(rot[...], which, NN_DIMS, preferred_element_type=f32)
        cos_t, sin_t = turn[:NT], turn[NT:]
        c_re = (r_re * cos_t - r_im * sin_t)[None]
        c_im = (r_re * sin_t + r_im * cos_t)[None]
        v = v.reshape(rows // NT, 2, NT, CHUNK)
        v_re, v_im = v[:, 0], v[:, 1]
        u_re = (c_re * v_re - c_im * v_im).reshape(rows, CHUNK)
        u_im = (c_re * v_im + c_im * v_re).reshape(rows, CHUNK)
        up_all[0:rows, pl.ds(at, CHUNK)] = u_re.astype(bf16)
        up_all[rows:rows2, pl.ds(at, CHUNK)] = u_im.astype(bf16)

    def product(at, size):
        return lax.dot_general(
            kv_all[:, pl.ds(at, size)],
            up_all[:, pl.ds(at, size)],
            NT_DIMS,
            preferred_element_type=f32,
        )

    def tile_column(tv, carry):
        group = tv // TVG * (NT * TVG) + tv % TVG
        merged[...] = jnp.zeros(merged.shape, f32)
        used = jnp.int32(0)
        for tu in range(NT):
            tile = group + tu * TVG
            holder = tile // per_dev
            local = tile % per_dev
            cell = jnp.concatenate([tiles[holder, local], jnp.zeros((8, 128), f32)], axis=1)
            at = pl.ds(pl.multiple_of(used // 128 * 128, 128), lanes + 128)
            merged[:, at] = merged[:, at] + pltpu.roll(cell, used % 128, axis=1)
            used = used + counts[0, local * devices + holder]
        chunks = (used + CHUNK - 1) // CHUNK

        if most == 8:
            low = -1
            for n in (2, 4, 5, 6, 8):

                @pl.when((chunks > low) & (chunks <= n))
                def _():
                    for i in range(n):
                        chunk(i * CHUNK)
                    grid[tv] = product(0, n * CHUNK).astype(bf16)

                low = n
        else:

            def make(i, c):
                chunk(pl.multiple_of(i * CHUNK, CHUNK))
                return c

            def add(i, ft):
                return ft + product(pl.multiple_of(i * CHUNK, CHUNK), CHUNK)

            lax.fori_loop(0, chunks, make, 0)
            ft = lax.fori_loop(0, chunks, add, jnp.zeros((side, rows2), f32))
            grid[tv] = ft.astype(bf16)
        return carry

    lax.fori_loop(0, NT, tile_column, 0)

    def stripe(j, carry):
        r0 = pl.multiple_of(j * 16, 16)
        tc = twist[0, pl.ds(r0, 16), :]
        ts = twist[1, pl.ds(r0, 16), :]
        for h in range(rows // width):
            c0 = h * width
            z = [
                (
                    grid[t, pl.ds(r0, 16), c0 : c0 + width].astype(f32),
                    grid[t, pl.ds(r0, 16), rows + c0 : rows + c0 + width].astype(f32),
                )
                for t in range(NT)
            ]
            x = fft_pos(z)
            for n0 in range(NT):
                re, im = x[n0]
                if n0 > 0:
                    c = tc[:, n0 : n0 + 1]
                    s = ts[:, n0 : n0 + 1]
                    re, im = re * c - im * s, re * s + im * c
                turned[n0, pl.ds(r0, 16), c0 : c0 + width] = re.astype(bf16)
                turned[n0, pl.ds(r0 + side, 16), c0 : c0 + width] = im.astype(bf16)
        return carry

    lax.fori_loop(0, side // 16, stripe, 0)

    for n0 in range(NT):
        x = lax.dot_general(turn_v[...], turned[n0], NN_DIMS, preferred_element_type=f32)
        for h in range(rows // width):
            flips[h][pl.ds(n0, side, stride=NT), :] = x[:, h * width : (h + 1) * width]

    pieces = sems.shape[0]
    wide = NPIX // pieces
    copies = []
    for i in range(pieces):
        for h in range(rows // width):
            stage[h * width : (h + 1) * width, i * wide : (i + 1) * wide] = (
                flips[h][i * wide : (i + 1) * wide, :].T
            )
        copy = pltpu.make_async_copy(
            stage.at[:, pl.ds(i * wide, wide)], out.at[:, pl.ds(i * wide, wide)], sems.at[i]
        )
        copy.start()
        copies.append(copy)
    for copy in copies:
        copy.wait()


def cos_sin(product, period):
    angle = (2.0 * math.pi / period) * (product % period).astype(f32)
    return jnp.cos(angle), jnp.sin(angle)


def exchange(x):
    return lax.all_to_all(x, AXES, split_axis=0, concat_axis=0, tiled=True)


def on_device(model_grid, vis_values, weights, flags, uv_frac, cell_offset, tile_index):
    devices = lax.axis_size("blen") * lax.axis_size("tm")
    me = lax.axis_index("blen") * lax.axis_size("tm") + lax.axis_index("tm")
    per_dev = model_grid.shape[0]
    side = model_grid.shape[2]
    n = weights.shape[0]
    ntiles = per_dev * devices
    lanes = devices * MOST
    rows = NPIX // devices
    call = pl.pallas_call
    shape = jax.ShapeDtypeStruct

    tile_row = tile_index.reshape(1, n)
    width = MOST * FIELDS * per_dev
    packed, rank = call(
        lambda *refs: pack_body(*refs, devices=devices, per_dev=per_dev),
        out_shape=(shape((devices, width), f32), shape((1, n), i32)),
        name="pack",
    )(tile_row, cell_offset, uv_frac, vis_values, weights.reshape(1, n), flags.reshape(1, n))
    recv = exchange(packed)
    image_rows = me * rows + jnp.arange(rows, dtype=i32)
    cells = jnp.arange(side, dtype=i32)
    small = jnp.arange(NT, dtype=i32)
    turn_u = cos_sin((image_rows[:, None] * cells[None, :]).reshape(rows // NT, NT, side), NPIX)
    turn_u = jnp.stack(turn_u, axis=1).reshape(2 * rows, side).astype(bf16)
    rot = cos_sin(small[:, None] * small[None, :], NT)
    rot = jnp.concatenate(split3(jnp.concatenate(rot)), axis=1)
    cos_v, sin_v = cos_sin(cells[:, None] * cells[None, :], side)
    turn_v = jnp.concatenate([cos_v, -sin_v], axis=1).astype(bf16)
    twist = jnp.stack(cos_sin(cells[:, None] * small[None, :], NPIX))
    recv, turn_u, rot, turn_v, twist = lax.optimization_barrier((recv, turn_u, rot, turn_v, twist))

    group = min(2, per_dev)
    sent, back = call(
        lambda *refs: predict_body(*refs, per_dev=per_dev),
        grid=(per_dev // group,),
        in_specs=[
            pl.BlockSpec((devices, width), lambda l: (0, 0)),
            pl.BlockSpec((group, 2, side, side), lambda l: (l, 0, 0, 0)),
        ],
        out_specs=(
            pl.BlockSpec((per_dev * SENT, lanes), lambda l: (0, 0)),
            pl.BlockSpec((devices, lanes), lambda l: (0, 0)),
        ),
        out_shape=(shape((per_dev * SENT, lanes), f32), shape((devices, lanes), f32)),
        scratch_shapes=[pltpu.VMEM((per_dev, FIELDS, lanes), f32)],
        compiler_params=params(32),
        name="predict",
    )(recv, pltpu.with_memory_space_constraint(model_grid, pltpu.HBM))
    sent = jnp.broadcast_to(sent[None], (devices,) + sent.shape)
    tiles = exchange(jnp.concatenate([sent, back[:, None, :]], axis=1))
    tiles = pltpu.with_memory_space_constraint(tiles, pltpu.HBM)

    thin = min(128, rows)
    vmem = pl.BlockSpec(memory_space=pltpu.VMEM)
    gradient, weighted_residual = call(
        image_body,
        in_specs=[vmem] * 7,
        out_specs=(pl.BlockSpec(memory_space=pl.ANY), vmem),
        out_shape=(shape((rows, NPIX), f32), shape((2, n), f32)),
        scratch_shapes=[
            pltpu.VMEM((devices, per_dev, 8, lanes), f32),
            pltpu.VMEM((8, NT * lanes + 128), f32),
            pltpu.VMEM((side, NT * lanes), bf16),
            pltpu.VMEM((2 * rows, NT * lanes), bf16),
            pltpu.VMEM((NT, side, 2 * rows), bf16),
            pltpu.VMEM((NT, 2 * side, rows), bf16),
            pltpu.VMEM((rows, NPIX), f32),
            pltpu.SemaphoreType.DMA((8,)),
            pltpu.VMEM((8, ntiles), i32),
            pltpu.SMEM((8, ntiles), i32),
        ]
        + [pltpu.VMEM((NPIX, thin), f32)] * (rows // thin),
        compiler_params=params(56),
        name="image",
    )(tiles, tile_row, rank, turn_u, rot, turn_v, twist)
    return (gradient, weighted_residual)


def solution(mesh):
    in_specs = (
        P(AXES, None, None, None),
        P(None, AXES),
        P(AXES),
        P(AXES),
        P(None, AXES),
        P(None, AXES),
        P(AXES, None),
    )
    out_specs = (P(AXES, None), P(None, AXES))
    return jax.shard_map(
        on_device, mesh=mesh, in_specs=in_specs, out_specs=out_specs, check_vma=False
    )
```

```python
import math

import jax
import jax.numpy as jnp
from jax import lax
from jax.experimental import pallas as pl
from jax.experimental.pallas import tpu as pltpu
from jax.sharding import Mesh
from jax.sharding import PartitionSpec as P

NPIX = 8192
KSUP = 8
NT = 16
TVG = 4
MOST = 4
FIELDS = 8
USED = 7
SENT = 6
CELLS = 16
CHUNK = 256

AXES = ("blen", "chip", "core")
CORES = 2
f32 = jnp.float32
bf16 = jnp.bfloat16
i32 = jnp.int32
NT_DIMS = (((1,), (1,)), ((), ()))
NN_DIMS = (((1,), (0,)), ((), ()))
MIB = 1 << 20


def params(mib):
    return pltpu.CompilerParams(vmem_limit_bytes=mib * MIB)


def split3(x):
    hi = x.astype(bf16)
    rest = x - hi.astype(f32)
    mid = rest.astype(bf16)
    low = (rest - mid.astype(f32)).astype(bf16)
    return hi, mid, low


def pattern(first, frac):
    cells = lax.broadcasted_iota(i32, (CELLS, first.shape[1]), 0)
    k = (cells - first) & (CELLS - 1)
    dist = (k - (KSUP // 2 - 1)).astype(f32) - frac
    value = jnp.where(k < KSUP, jnp.exp(-0.5 * dist * dist), 0.0).astype(bf16)
    return value, ((first + k) >> 4).astype(f32).astype(bf16)


def dense(value, where, side):
    zero = jnp.zeros_like(value)
    blocks = [jnp.where(where == jnp.bfloat16(b), value, zero) for b in range(side // CELLS)]
    return jnp.concatenate(blocks, axis=0)


def pack_body(tile_row, offset, frac, vis, weight, flag, packed, rank_out, *, devices, per_dev):
    n = tile_row.shape[1]
    t_row = tile_row[...]
    across = jnp.broadcast_to(t_row.astype(f32), (128, n)).T
    parts = []
    for c in range(n // 128):
        part = t_row[:, c * 128 : (c + 1) * 128].astype(f32)
        before = lax.broadcasted_iota(i32, (n, 128), 0)
        before = before < lax.broadcasted_iota(i32, (n, 128), 1) + c * 128
        same = jnp.where((across == part) & before, 1.0, 0.0)
        parts.append(jnp.sum(same, axis=0, keepdims=True))
    rank = jnp.concatenate(parts, axis=1).astype(i32)
    rank_out[...] = rank
    owner = t_row // per_dev
    local = t_row - owner * per_dev
    owners = lax.broadcasted_iota(i32, (devices, n), 0) == owner
    places = MOST * per_dev
    hot = lax.broadcasted_iota(i32, (places, n), 0) == rank * per_dev + local
    hot = hot.astype(f32).astype(bf16)
    rows = [
        offset[0:1, :].astype(f32),
        offset[1:2, :].astype(f32),
        frac[0:1, :],
        frac[1:2, :],
        vis[0:1, :],
        vis[1:2, :],
        weight[...] * flag[...].astype(f32),
    ]
    packed[...] = jnp.zeros(packed.shape, f32)
    for f in range(USED):
        spread = jnp.where(owners, rows[f], 0.0)
        total = jnp.zeros((devices, places), f32)
        for part in split3(spread):
            total = total + lax.dot_general(part, hot, NT_DIMS, preferred_element_type=f32)
        for k in range(MOST):
            at = (k * FIELDS + f) * per_dev
            packed[:, 0, at : at + per_dev] = total[:, k * per_dev : (k + 1) * per_dev]


def predict_body(recv, model, sent, back, fields, flip, *, per_dev):
    group = model.shape[0]
    side = model.shape[2]
    lanes = sent.shape[1]
    devices = recv.shape[0]
    step = pl.program_id(0)

    @pl.when(step == 0)
    def _():
        turned = recv[...].T
        span = FIELDS * per_dev
        for k in range(MOST):
            some = turned[k * span : (k + 1) * span, :]
            for t in range(per_dev):
                for f in range(FIELDS):
                    at = f * per_dev + t
                    fields[t, f : f + 1, k * devices : (k + 1) * devices] = some[at : at + 1, :]

    for i in range(group):
        l = step * group + i
        rows = fields[l]
        first = rows[0:2].astype(i32) - (KSUP // 2 - 1)
        ku = dense(*pattern(first[0:1], rows[2:3]), side)
        kv = dense(*pattern(first[1:2], rows[3:4]), side).astype(f32)
        for c in range(2):
            product = lax.dot_general(model[i, c], ku, NN_DIMS, preferred_element_type=f32)
            predicted = jnp.sum(product * kv, axis=0, keepdims=True)
            fields[l, 4 + c : 5 + c, :] = rows[6:7] * (predicted - rows[4 + c : 5 + c])

    @pl.when(step == per_dev // group - 1)
    def _():
        above = lax.broadcasted_iota(i32, (lanes, lanes), 0)
        above = above < lax.broadcasted_iota(i32, (lanes, lanes), 1)
        above = above.astype(f32).astype(bf16)
        there = jnp.concatenate([fields[t, 0:1, :] for t in range(per_dev)], axis=0) > 0.5
        place = lax.dot_general(
            there.astype(f32).astype(bf16), above, NN_DIMS, preferred_element_type=f32
        )
        place = jnp.where(there, place, -1.0).astype(i32)
        for t in range(per_dev):
            move = lax.broadcasted_iota(i32, (lanes, lanes), 0) == place[t : t + 1]
            move = move.astype(f32).astype(bf16)
            parts = jnp.concatenate(split3(fields[t]), axis=0)
            total = lax.dot_general(parts, move, NT_DIMS, preferred_element_type=f32)
            total = total[0:8] + total[8:16] + total[16:24]
            sent[t * SENT : (t + 1) * SENT, :] = total[0:SENT]
        mine = [fields[t, 4 + c : 5 + c, :] for c in range(2) for t in range(per_dev)]
        wide = 2 * per_dev
        flip[:, 0:wide] = jnp.concatenate(mine, axis=0).T
        back[...] = jnp.zeros(back.shape, f32)
        for core in range(CORES):
            for k in range(MOST):
                some = flip[pl.ds(k * devices + core, devices // CORES, stride=CORES), :]
                at = (core * MOST + k) * wide
                back[:, at : at + wide] = some[:, 0:wide]


def fft_pos(z):
    n = len(z)
    if n == 1:
        return z
    even = fft_pos(z[0::2])
    odd = fft_pos(z[1::2])
    low, high = [], []
    for k in range(n // 2):
        o_re, o_im = odd[k]
        if k == 0:
            t_re, t_im = o_re, o_im
        elif 4 * k == n:
            t_re, t_im = -o_im, o_re
        else:
            c, s = math.cos(2 * math.pi * k / n), math.sin(2 * math.pi * k / n)
            t_re = o_re * c - o_im * s
            t_im = o_re * s + o_im * c
        e_re, e_im = even[k]
        low.append((e_re + t_re, e_im + t_im))
        high.append((e_re - t_re, e_im - t_im))
    return low + high


def image_body(
    core, near, far, tile_row, rank, turn_u, rot, turn_v, twist, out, own,
    tiles, merged, kv_all, up_all, grid, turned, stage, sems, tally, counts, *flips,
):
    side = turn_u.shape[1]
    rows2 = turn_u.shape[0]
    rows = rows2 // 2
    chips = near.shape[0]
    lanes = near.shape[2]
    per_dev = near.shape[1] // SENT
    width = flips[0].shape[1]
    most = NT * lanes // CHUNK

    there = []
    for far_off, recv in enumerate((near, far)):
        from_core = core[0] if far_off == 0 else 1 - core[0]
        for l in range(per_dev):
            some = recv[:, l * SENT : (l + 1) * SENT, :]
            filled = some[:, 0:1, :] > 0.5
            owner = lax.broadcasted_iota(i32, filled.shape, 0) * CORES + from_core
            tile = owner * per_dev + l
            mark = jnp.where(filled, (tile // TVG % NT).astype(f32), 0.0)
            tiles[far_off, l] = jnp.concatenate([some, mark, jnp.zeros_like(mark)], axis=1)
            there.append(jnp.where(filled[:, 0], 1.0, 0.0).astype(bf16))
    total = lax.dot_general(
        jnp.ones((8, lanes), bf16),
        jnp.concatenate(there, axis=0),
        NT_DIMS,
        preferred_element_type=f32,
    )
    tally[...] = total.astype(i32)
    count_copy = pltpu.make_async_copy(tally, counts, sems.at[0])
    count_copy.start()

    n = tile_row.shape[1]
    t_row = tile_row[...]
    owner = t_row // per_dev
    local = t_row - owner * per_dev
    span = MOST * 2 * per_dev
    total = jnp.zeros((3 * lanes, n), f32)
    for far_off, recv in enumerate((near, far)):
        from_core = core[0] if far_off == 0 else 1 - core[0]
        hot = lax.broadcasted_iota(i32, (chips, n), 0) * CORES + from_core == owner
        hot = hot.astype(f32).astype(bf16)
        mine = jnp.concatenate(split3(recv[:, per_dev * SENT, :].T), axis=0)
        total = total + lax.dot_general(mine, hot, NN_DIMS, preferred_element_type=f32)
    total = total[0:lanes] + total[lanes : 2 * lanes] + total[2 * lanes : 3 * lanes]
    places = lax.broadcasted_iota(i32, (lanes, n), 0)
    for c in range(2):
        picked = places == core[0] * span + (rank[...] * 2 + c) * per_dev + local
        own[c : c + 1, :] = jnp.sum(jnp.where(picked, total, 0.0), axis=0, keepdims=True)
    count_copy.wait()

    def chunk(at):
        m = merged[:, pl.ds(at, CHUNK)]
        first = m[0:2].astype(i32) - (KSUP // 2 - 1)
        ku = dense(*pattern(first[0:1], m[2:3]), side)
        kv_all[:, pl.ds(at, CHUNK)] = dense(*pattern(first[1:2], m[3:4]), side)
        v = lax.dot_general(turn_u[...], ku, NN_DIMS, preferred_element_type=f32)
        r_re = m[4:5] * (1.0 / NPIX)
        r_im = m[5:6] * (1.0 / NPIX)
        which = lax.broadcasted_iota(i32, (NT, CHUNK), 0).astype(f32) == m[6:7]
        which = which.astype(f32).astype(bf16)
        which = jnp.concatenate([which] * 3, axis=0)
        turn = lax.dot_general(rot[...], which, NN_DIMS, preferred_element_type=f32)
        cos_t, sin_t = turn[:NT], turn[NT:]
        c_re = (r_re * cos_t - r_im * sin_t)[None]
        c_im = (r_re * sin_t + r_im * cos_t)[None]
        v = v.reshape(rows // NT, 2, NT, CHUNK)
        v_re, v_im = v[:, 0], v[:, 1]
        u_re = (c_re * v_re - c_im * v_im).reshape(rows, CHUNK)
        u_im = (c_re * v_im + c_im * v_re).reshape(rows, CHUNK)
        up_all[0:rows, pl.ds(at, CHUNK)] = u_re.astype(bf16)
        up_all[rows:rows2, pl.ds(at, CHUNK)] = u_im.astype(bf16)

    def product(at, size):
        return lax.dot_general(
            kv_all[:, pl.ds(at, size)],
            up_all[:, pl.ds(at, size)],
            NT_DIMS,
            preferred_element_type=f32,
        )

    def tile_column(tv, carry):
        group = tv // TVG * (NT * TVG) + tv % TVG
        merged[...] = jnp.zeros(merged.shape, f32)
        used = jnp.int32(0)
        for tu in range(NT):
            tile = group + tu * TVG
            owner = tile // per_dev
            local = tile % per_dev
            far_off = (owner + core[0]) % CORES
            chip = owner // CORES
            cell = tiles[far_off, local, chip]
            cell = jnp.concatenate([cell, jnp.zeros((8, 128), f32)], axis=1)
            at = pl.ds(pl.multiple_of(used // 128 * 128, 128), lanes + 128)
            merged[:, at] = merged[:, at] + pltpu.roll(cell, used % 128, axis=1)
            used = used + counts[0, (far_off * per_dev + local) * chips + chip]
        chunks = (used + CHUNK - 1) // CHUNK

        if most == 8:
            low = -1
            for n in (2, 4, 5, 6, 8):

                @pl.when((chunks > low) & (chunks <= n))
                def _():
                    for i in range(n):
                        chunk(i * CHUNK)
                    grid[tv] = product(0, n * CHUNK).astype(bf16)

                low = n
        else:

            def make(i, c):
                chunk(pl.multiple_of(i * CHUNK, CHUNK))
                return c

            def add(i, ft):
                return ft + product(pl.multiple_of(i * CHUNK, CHUNK), CHUNK)

            lax.fori_loop(0, chunks, make, 0)
            ft = lax.fori_loop(0, chunks, add, jnp.zeros((side, rows2), f32))
            grid[tv] = ft.astype(bf16)
        return carry

    lax.fori_loop(0, NT, tile_column, 0)

    def stripe(j, carry):
        r0 = pl.multiple_of(j * 16, 16)
        tc = twist[0, pl.ds(r0, 16), :]
        ts = twist[1, pl.ds(r0, 16), :]
        for h in range(rows // width):
            c0 = h * width
            z = [
                (
                    grid[t, pl.ds(r0, 16), c0 : c0 + width].astype(f32),
                    grid[t, pl.ds(r0, 16), rows + c0 : rows + c0 + width].astype(f32),
                )
                for t in range(NT)
            ]
            x = fft_pos(z)
            for n0 in range(NT):
                re, im = x[n0]
                if n0 > 0:
                    c = tc[:, n0 : n0 + 1]
                    s = ts[:, n0 : n0 + 1]
                    re, im = re * c - im * s, re * s + im * c
                turned[n0, pl.ds(r0, 16), c0 : c0 + width] = re.astype(bf16)
                turned[n0, pl.ds(r0 + side, 16), c0 : c0 + width] = im.astype(bf16)
        return carry

    lax.fori_loop(0, side // 16, stripe, 0)

    for n0 in range(NT):
        x = lax.dot_general(turn_v[...], turned[n0], NN_DIMS, preferred_element_type=f32)
        for h in range(rows // width):
            flips[h][pl.ds(n0, side, stride=NT), :] = x[:, h * width : (h + 1) * width]

    pieces = sems.shape[0]
    wide = NPIX // pieces
    copies = []
    for i in range(pieces):
        for h in range(rows // width):
            stage[h * width : (h + 1) * width, i * wide : (i + 1) * wide] = (
                flips[h][i * wide : (i + 1) * wide, :].T
            )
        copy = pltpu.make_async_copy(
            stage.at[:, pl.ds(i * wide, wide)], out.at[:, pl.ds(i * wide, wide)], sems.at[i]
        )
        copy.start()
        copies.append(copy)
    for copy in copies:
        copy.wait()


def cos_sin(product, period):
    angle = (2.0 * math.pi / period) * (product % period).astype(f32)
    return jnp.cos(angle), jnp.sin(angle)


def on_device(model_grid, vis_values, weights, flags, uv_frac, cell_offset, tile_index):
    chips = lax.axis_size("blen") * lax.axis_size("chip")
    devices = chips * CORES
    core = lax.axis_index("core")
    me = (lax.axis_index("blen") * lax.axis_size("chip") + lax.axis_index("chip")) * CORES + core
    per_dev = model_grid.shape[0]
    side = model_grid.shape[2]
    n = weights.shape[0]
    ntiles = per_dev * devices
    lanes = devices * MOST
    rows = NPIX // devices
    call = pl.pallas_call
    shape = jax.ShapeDtypeStruct

    tile_row = tile_index.reshape(1, n)
    width = MOST * FIELDS * per_dev
    packed, rank = call(
        lambda *refs: pack_body(*refs, devices=devices, per_dev=per_dev),
        out_shape=(shape((devices, 1, width), f32), shape((1, n), i32)),
        name="pack",
    )(tile_row, cell_offset, uv_frac, vis_values, weights.reshape(1, n), flags.reshape(1, n))
    recv = lax.all_to_all(packed, AXES, split_axis=0, concat_axis=0, tiled=True)
    recv = recv.reshape(devices, width)
    image_rows = me * rows + jnp.arange(rows, dtype=i32)
    cells = jnp.arange(side, dtype=i32)
    small = jnp.arange(NT, dtype=i32)
    turn_u = cos_sin((image_rows[:, None] * cells[None, :]).reshape(rows // NT, NT, side), NPIX)
    turn_u = jnp.stack(turn_u, axis=1).reshape(2 * rows, side).astype(bf16)
    rot = cos_sin(small[:, None] * small[None, :], NT)
    rot = jnp.concatenate(split3(jnp.concatenate(rot)), axis=1)
    cos_v, sin_v = cos_sin(cells[:, None] * cells[None, :], side)
    turn_v = jnp.concatenate([cos_v, -sin_v], axis=1).astype(bf16)
    twist = jnp.stack(cos_sin(cells[:, None] * small[None, :], NPIX))
    recv, turn_u, rot, twist = lax.optimization_barrier((recv, turn_u, rot, twist))

    group = min(2, per_dev)
    sent, back = call(
        lambda *refs: predict_body(*refs, per_dev=per_dev),
        grid=(per_dev // group,),
        in_specs=[
            pl.BlockSpec((devices, width), lambda l: (0, 0)),
            pl.BlockSpec((group, 2, side, side), lambda l: (l, 0, 0, 0)),
        ],
        out_specs=(
            pl.BlockSpec((per_dev * SENT, lanes), lambda l: (0, 0)),
            pl.BlockSpec((chips, lanes), lambda l: (0, 0)),
        ),
        out_shape=(shape((per_dev * SENT, lanes), f32), shape((chips, lanes), f32)),
        scratch_shapes=[pltpu.VMEM((per_dev, FIELDS, lanes), f32), pltpu.VMEM((lanes, 128), f32)],
        compiler_params=params(32),
        name="predict",
    )(recv, pltpu.with_memory_space_constraint(model_grid, pltpu.HBM))
    sent = jnp.broadcast_to(sent[None], (chips,) + sent.shape)
    near = lax.all_to_all(
        jnp.concatenate([sent, back[:, None, :]], axis=1),
        AXES[:2],
        split_axis=0,
        concat_axis=0,
        tiled=True,
    )
    near, turn_v, twist = lax.optimization_barrier((near, turn_v, twist))
    far = lax.ppermute(near, "core", [(0, 1), (1, 0)])

    thin = min(128, rows)
    vmem = pl.BlockSpec(memory_space=pltpu.VMEM)
    gradient, weighted_residual = call(
        image_body,
        in_specs=[pl.BlockSpec(memory_space=pltpu.SMEM)] + [vmem] * 8,
        out_specs=(pl.BlockSpec(memory_space=pl.ANY), vmem),
        out_shape=(shape((rows, NPIX), f32), shape((2, n), f32)),
        scratch_shapes=[
            pltpu.VMEM((CORES, per_dev, chips, 8, lanes), f32),
            pltpu.VMEM((8, NT * lanes + 128), f32),
            pltpu.VMEM((side, NT * lanes), bf16),
            pltpu.VMEM((2 * rows, NT * lanes), bf16),
            pltpu.VMEM((NT, side, 2 * rows), bf16),
            pltpu.VMEM((NT, 2 * side, rows), bf16),
            pltpu.VMEM((rows, NPIX), f32),
            pltpu.SemaphoreType.DMA((8,)),
            pltpu.VMEM((8, ntiles), i32),
            pltpu.SMEM((8, ntiles), i32),
        ]
        + [pltpu.VMEM((NPIX, thin), f32)] * (rows // thin),
        compiler_params=params(44),
        name="image",
    )(core.reshape(1), near, far, tile_row, rank, turn_u, rot, turn_v, twist)
    return (gradient, weighted_residual)


def solution(mesh):
    cut = mesh.devices.reshape(mesh.shape["blen"], mesh.shape["tm"] // CORES, CORES)
    whole = P(AXES)
    in_specs = (
        P(AXES, None, None, None),
        P(None, AXES),
        whole,
        whole,
        P(None, AXES),
        P(None, AXES),
        P(AXES, None),
    )
    out_specs = (P(AXES, None), P(None, AXES))
    return jax.shard_map(
        on_device, mesh=Mesh(cut, AXES), in_specs=in_specs, out_specs=out_specs, check_vma=False
    )
```

```python
import math

import jax
import jax.numpy as jnp
from jax import lax
from jax.experimental import pallas as pl
from jax.experimental.pallas import tpu as pltpu
from jax.sharding import Mesh
from jax.sharding import PartitionSpec as P

NPIX = 8192
KSUP = 8
NT = 16
TVG = 4
MOST = 4
FIELDS = 8
USED = 7
SENT = 6
CELLS = 16
CHUNK = 256

AXES = ("blen", "chip", "core")
CORES = 2
f32 = jnp.float32
bf16 = jnp.bfloat16
i32 = jnp.int32
NT_DIMS = (((1,), (1,)), ((), ()))
NN_DIMS = (((1,), (0,)), ((), ()))
MIB = 1 << 20


def params(mib):
    return pltpu.CompilerParams(vmem_limit_bytes=mib * MIB)


def split3(x):
    hi = x.astype(bf16)
    rest = x - hi.astype(f32)
    mid = rest.astype(bf16)
    low = (rest - mid.astype(f32)).astype(bf16)
    return hi, mid, low


def pattern(first, frac):
    cells = lax.broadcasted_iota(i32, (CELLS, first.shape[1]), 0)
    k = (cells - first) & (CELLS - 1)
    dist = (k - (KSUP // 2 - 1)).astype(f32) - frac
    value = jnp.where(k < KSUP, jnp.exp(-0.5 * dist * dist), 0.0).astype(bf16)
    return value, ((first + k) >> 4).astype(f32).astype(bf16)


def dense(value, where, side):
    zero = jnp.zeros_like(value)
    blocks = [jnp.where(where == jnp.bfloat16(b), value, zero) for b in range(side // CELLS)]
    return jnp.concatenate(blocks, axis=0)


def pack_body(tile_row, offset, frac, vis, weight, flag, packed, rank_out, *, devices, per_dev):
    n = tile_row.shape[1]
    t_row = tile_row[...]
    across = jnp.broadcast_to(t_row.astype(f32), (128, n)).T
    parts = []
    for c in range(n // 128):
        part = t_row[:, c * 128 : (c + 1) * 128].astype(f32)
        before = lax.broadcasted_iota(i32, (n, 128), 0)
        before = before < lax.broadcasted_iota(i32, (n, 128), 1) + c * 128
        same = jnp.where((across == part) & before, 1.0, 0.0)
        parts.append(jnp.sum(same, axis=0, keepdims=True))
    rank = jnp.concatenate(parts, axis=1).astype(i32)
    rank_out[...] = rank
    owner = t_row // per_dev
    local = t_row - owner * per_dev
    owners = lax.broadcasted_iota(i32, (devices, n), 0) == owner
    places = MOST * per_dev
    hot = lax.broadcasted_iota(i32, (places, n), 0) == rank * per_dev + local
    hot = hot.astype(f32).astype(bf16)
    rows = [
        offset[0:1, :].astype(f32),
        offset[1:2, :].astype(f32),
        frac[0:1, :],
        frac[1:2, :],
        vis[0:1, :],
        vis[1:2, :],
        weight[...] * flag[...].astype(f32),
    ]
    packed[...] = jnp.zeros(packed.shape, f32)
    for f in range(USED):
        spread = jnp.where(owners, rows[f], 0.0)
        total = jnp.zeros((devices, places), f32)
        for part in split3(spread):
            total = total + lax.dot_general(part, hot, NT_DIMS, preferred_element_type=f32)
        for k in range(MOST):
            at = (k * FIELDS + f) * per_dev
            packed[:, 0, at : at + per_dev] = total[:, k * per_dev : (k + 1) * per_dev]


def predict_body(recv, model, sent, back, fields, flip, *, per_dev):
    group = model.shape[0]
    side = model.shape[2]
    lanes = sent.shape[1]
    devices = recv.shape[0]
    step = pl.program_id(0)

    @pl.when(step == 0)
    def _():
        turned = recv[...].T
        span = FIELDS * per_dev
        for k in range(MOST):
            some = turned[k * span : (k + 1) * span, :]
            for t in range(per_dev):
                for f in range(FIELDS):
                    at = f * per_dev + t
                    fields[t, f : f + 1, k * devices : (k + 1) * devices] = some[at : at + 1, :]

    for i in range(group):
        l = step * group + i
        rows = fields[l]
        first = rows[0:2].astype(i32) - (KSUP // 2 - 1)
        ku = dense(*pattern(first[0:1], rows[2:3]), side)
        kv = dense(*pattern(first[1:2], rows[3:4]), side).astype(f32)
        for c in range(2):
            product = lax.dot_general(model[i, c], ku, NN_DIMS, preferred_element_type=f32)
            predicted = jnp.sum(product * kv, axis=0, keepdims=True)
            fields[l, 4 + c : 5 + c, :] = rows[6:7] * (predicted - rows[4 + c : 5 + c])

    @pl.when(step == per_dev // group - 1)
    def _():
        above = lax.broadcasted_iota(i32, (lanes, lanes), 0)
        above = above < lax.broadcasted_iota(i32, (lanes, lanes), 1)
        above = above.astype(f32).astype(bf16)
        there = jnp.concatenate([fields[t, 0:1, :] for t in range(per_dev)], axis=0) > 0.5
        place = lax.dot_general(
            there.astype(f32).astype(bf16), above, NN_DIMS, preferred_element_type=f32
        )
        place = jnp.where(there, place, -1.0).astype(i32)
        for t in range(per_dev):
            move = lax.broadcasted_iota(i32, (lanes, lanes), 0) == place[t : t + 1]
            move = move.astype(f32).astype(bf16)
            parts = jnp.concatenate(split3(fields[t]), axis=0)
            total = lax.dot_general(parts, move, NT_DIMS, preferred_element_type=f32)
            total = total[0:8] + total[8:16] + total[16:24]
            sent[t * SENT : (t + 1) * SENT, :] = total[0:SENT]
        mine = [fields[t, 4 + c : 5 + c, :] for c in range(2) for t in range(per_dev)]
        wide = 2 * per_dev
        flip[:, 0:wide] = jnp.concatenate(mine, axis=0).T
        back[...] = jnp.zeros(back.shape, f32)
        for core in range(CORES):
            for k in range(MOST):
                some = flip[pl.ds(k * devices + core, devices // CORES, stride=CORES), :]
                at = (core * MOST + k) * wide
                back[:, at : at + wide] = some[:, 0:wide]


def fft_pos(z):
    n = len(z)
    if n == 1:
        return z
    even = fft_pos(z[0::2])
    odd = fft_pos(z[1::2])
    low, high = [], []
    for k in range(n // 2):
        o_re, o_im = odd[k]
        if k == 0:
            t_re, t_im = o_re, o_im
        elif 4 * k == n:
            t_re, t_im = -o_im, o_re
        else:
            c, s = math.cos(2 * math.pi * k / n), math.sin(2 * math.pi * k / n)
            t_re = o_re * c - o_im * s
            t_im = o_re * s + o_im * c
        e_re, e_im = even[k]
        low.append((e_re + t_re, e_im + t_im))
        high.append((e_re - t_re, e_im - t_im))
    return low + high


def image_body(
    core, near, far, tile_row, rank, turn_u, rot, turn_v, twist, out, own,
    tiles, merged, kv_all, up_all, grid, turned, stage, sems, tally, counts, *flips,
):
    side = turn_u.shape[1]
    rows2 = turn_u.shape[0]
    rows = rows2 // 2
    chips = near.shape[0]
    lanes = near.shape[2]
    per_dev = near.shape[1] // SENT
    width = flips[0].shape[1]
    most = NT * lanes // CHUNK

    for far_off, recv in enumerate((near, far)):
        from_core = core[0] if far_off == 0 else 1 - core[0]
        for l in range(per_dev):
            some = recv[:, l * SENT : (l + 1) * SENT, :]
            owner = lax.broadcasted_iota(i32, (chips, 1, lanes), 0) * CORES + from_core
            mark = ((owner * per_dev + l) // TVG % NT).astype(f32)
            mark = jnp.where(some[:, 0:1, :] > 0.5, mark, 0.0)
            cells = jnp.concatenate([some, mark, jnp.zeros_like(mark)], axis=1)
            for chip in range(chips):
                tiles[(chip * CORES + from_core) * per_dev + l] = cells[chip]
    there = jnp.where(tiles[:, 0, :] > 0.5, 1.0, 0.0).astype(bf16)
    total = lax.dot_general(
        jnp.ones((8, lanes), bf16),
        there,
        NT_DIMS,
        preferred_element_type=f32,
    )
    tally[...] = total.astype(i32)
    count_copy = pltpu.make_async_copy(tally, counts, sems.at[0])
    count_copy.start()

    n = tile_row.shape[1]
    t_row = tile_row[...]
    owner = t_row // per_dev
    local = t_row - owner * per_dev
    span = MOST * 2 * per_dev
    total = jnp.zeros((3 * lanes, n), f32)
    for far_off, recv in enumerate((near, far)):
        from_core = core[0] if far_off == 0 else 1 - core[0]
        hot = lax.broadcasted_iota(i32, (chips, n), 0) * CORES + from_core == owner
        hot = hot.astype(f32).astype(bf16)
        mine = jnp.concatenate(split3(recv[:, per_dev * SENT, :].T), axis=0)
        total = total + lax.dot_general(mine, hot, NN_DIMS, preferred_element_type=f32)
    total = total[0:lanes] + total[lanes : 2 * lanes] + total[2 * lanes : 3 * lanes]
    places = lax.broadcasted_iota(i32, (lanes, n), 0)
    for c in range(2):
        picked = places == core[0] * span + (rank[...] * 2 + c) * per_dev + local
        own[c : c + 1, :] = jnp.sum(jnp.where(picked, total, 0.0), axis=0, keepdims=True)
    count_copy.wait()

    def chunk(at):
        m = merged[:, pl.ds(at, CHUNK)]
        first = m[0:2].astype(i32) - (KSUP // 2 - 1)
        ku = dense(*pattern(first[0:1], m[2:3]), side)
        kv_all[:, pl.ds(at, CHUNK)] = dense(*pattern(first[1:2], m[3:4]), side)
        v = lax.dot_general(turn_u[...], ku, NN_DIMS, preferred_element_type=f32)
        r_re = m[4:5] * (1.0 / NPIX)
        r_im = m[5:6] * (1.0 / NPIX)
        which = lax.broadcasted_iota(i32, (NT, CHUNK), 0).astype(f32) == m[6:7]
        which = which.astype(f32).astype(bf16)
        which = jnp.concatenate([which] * 3, axis=0)
        turn = lax.dot_general(rot[...], which, NN_DIMS, preferred_element_type=f32)
        cos_t, sin_t = turn[:NT], turn[NT:]
        c_re = (r_re * cos_t - r_im * sin_t)[None]
        c_im = (r_re * sin_t + r_im * cos_t)[None]
        v = v.reshape(rows // NT, 2, NT, CHUNK)
        v_re, v_im = v[:, 0], v[:, 1]
        u_re = (c_re * v_re - c_im * v_im).reshape(rows, CHUNK)
        u_im = (c_re * v_im + c_im * v_re).reshape(rows, CHUNK)
        up_all[0:rows, pl.ds(at, CHUNK)] = u_re.astype(bf16)
        up_all[rows:rows2, pl.ds(at, CHUNK)] = u_im.astype(bf16)

    def product(at, size):
        return lax.dot_general(
            kv_all[:, pl.ds(at, size)],
            up_all[:, pl.ds(at, size)],
            NT_DIMS,
            preferred_element_type=f32,
        )

    def tile_column(tv, carry):
        group = (tv >> 2) * (NT * TVG) + (tv & 3)
        merged[...] = jnp.zeros(merged.shape, f32)
        used = jnp.int32(0)
        for tu in range(NT):
            tile = group + tu * TVG
            cell = jnp.concatenate([tiles[tile], jnp.zeros((8, 128), f32)], axis=1)
            at = pl.ds(pl.multiple_of((used >> 7) << 7, 128), lanes + 128)
            merged[:, at] = merged[:, at] + pltpu.roll(cell, used & 127, axis=1)
            used = used + counts[0, tile]
        chunks = (used + CHUNK - 1) // CHUNK

        if most == 8:
            low = -1
            for n in (2, 4, 5, 6, 8):

                @pl.when((chunks > low) & (chunks <= n))
                def _():
                    for i in range(n):
                        chunk(i * CHUNK)
                    grid[tv] = product(0, n * CHUNK).astype(bf16)

                low = n
        else:

            def make(i, c):
                chunk(pl.multiple_of(i * CHUNK, CHUNK))
                return c

            def add(i, ft):
                return ft + product(pl.multiple_of(i * CHUNK, CHUNK), CHUNK)

            lax.fori_loop(0, chunks, make, 0)
            ft = lax.fori_loop(0, chunks, add, jnp.zeros((side, rows2), f32))
            grid[tv] = ft.astype(bf16)
        return carry

    lax.fori_loop(0, NT, tile_column, 0)

    def stripe(j, carry):
        r0 = pl.multiple_of(j * 16, 16)
        tc = twist[0, pl.ds(r0, 16), :]
        ts = twist[1, pl.ds(r0, 16), :]
        for h in range(rows // width):
            c0 = h * width
            z = [
                (
                    grid[t, pl.ds(r0, 16), c0 : c0 + width].astype(f32),
                    grid[t, pl.ds(r0, 16), rows + c0 : rows + c0 + width].astype(f32),
                )
                for t in range(NT)
            ]
            x = fft_pos(z)
            for n0 in range(NT):
                re, im = x[n0]
                if n0 > 0:
                    c = tc[:, n0 : n0 + 1]
                    s = ts[:, n0 : n0 + 1]
                    re, im = re * c - im * s, re * s + im * c
                turned[n0, pl.ds(r0, 16), c0 : c0 + width] = re.astype(bf16)
                turned[n0, pl.ds(r0 + side, 16), c0 : c0 + width] = im.astype(bf16)
        return carry

    lax.fori_loop(0, side // 16, stripe, 0)

    for n0 in range(NT):
        x = lax.dot_general(turn_v[...], turned[n0], NN_DIMS, preferred_element_type=f32)
        for h in range(rows // width):
            flips[h][pl.ds(n0, side, stride=NT), :] = x[:, h * width : (h + 1) * width]

    pieces = sems.shape[0]
    wide = NPIX // pieces
    copies = []
    for i in range(pieces):
        for h in range(rows // width):
            stage[h * width : (h + 1) * width, i * wide : (i + 1) * wide] = (
                flips[h][i * wide : (i + 1) * wide, :].T
            )
        copy = pltpu.make_async_copy(
            stage.at[:, pl.ds(i * wide, wide)], out.at[:, pl.ds(i * wide, wide)], sems.at[i]
        )
        copy.start()
        copies.append(copy)
    for copy in copies:
        copy.wait()


def cos_sin(product, period):
    angle = (2.0 * math.pi / period) * (product % period).astype(f32)
    return jnp.cos(angle), jnp.sin(angle)


def on_device(model_grid, vis_values, weights, flags, uv_frac, cell_offset, tile_index):
    chips = lax.axis_size("blen") * lax.axis_size("chip")
    devices = chips * CORES
    core = lax.axis_index("core")
    me = (lax.axis_index("blen") * lax.axis_size("chip") + lax.axis_index("chip")) * CORES + core
    per_dev = model_grid.shape[0]
    side = model_grid.shape[2]
    n = weights.shape[0]
    ntiles = per_dev * devices
    lanes = devices * MOST
    rows = NPIX // devices
    call = pl.pallas_call
    shape = jax.ShapeDtypeStruct

    tile_row = tile_index.reshape(1, n)
    width = MOST * FIELDS * per_dev
    packed, rank = call(
        lambda *refs: pack_body(*refs, devices=devices, per_dev=per_dev),
        out_shape=(shape((devices, 1, width), f32), shape((1, n), i32)),
        name="pack",
    )(tile_row, cell_offset, uv_frac, vis_values, weights.reshape(1, n), flags.reshape(1, n))
    recv = lax.all_to_all(packed, AXES, split_axis=0, concat_axis=0, tiled=True)
    recv = recv.reshape(devices, width)
    image_rows = me * rows + jnp.arange(rows, dtype=i32)
    cells = jnp.arange(side, dtype=i32)
    small = jnp.arange(NT, dtype=i32)
    turn_u = cos_sin((image_rows[:, None] * cells[None, :]).reshape(rows // NT, NT, side), NPIX)
    turn_u = jnp.stack(turn_u, axis=1).reshape(2 * rows, side).astype(bf16)
    rot = cos_sin(small[:, None] * small[None, :], NT)
    rot = jnp.concatenate(split3(jnp.concatenate(rot)), axis=1)
    cos_v, sin_v = cos_sin(cells[:, None] * cells[None, :], side)
    turn_v = jnp.concatenate([cos_v, -sin_v], axis=1).astype(bf16)
    twist = jnp.stack(cos_sin(cells[:, None] * small[None, :], NPIX))
    recv, turn_u, rot, twist = lax.optimization_barrier((recv, turn_u, rot, twist))

    group = min(2, per_dev)
    sent, back = call(
        lambda *refs: predict_body(*refs, per_dev=per_dev),
        grid=(per_dev // group,),
        in_specs=[
            pl.BlockSpec((devices, width), lambda l: (0, 0)),
            pl.BlockSpec((group, 2, side, side), lambda l: (l, 0, 0, 0)),
        ],
        out_specs=(
            pl.BlockSpec((per_dev * SENT, lanes), lambda l: (0, 0)),
            pl.BlockSpec((chips, lanes), lambda l: (0, 0)),
        ),
        out_shape=(shape((per_dev * SENT, lanes), f32), shape((chips, lanes), f32)),
        scratch_shapes=[pltpu.VMEM((per_dev, FIELDS, lanes), f32), pltpu.VMEM((lanes, 128), f32)],
        compiler_params=params(32),
        name="predict",
    )(recv, pltpu.with_memory_space_constraint(model_grid, pltpu.HBM))
    sent = jnp.broadcast_to(sent[None], (chips,) + sent.shape)
    near = lax.all_to_all(
        jnp.concatenate([sent, back[:, None, :]], axis=1),
        AXES[:2],
        split_axis=0,
        concat_axis=0,
        tiled=True,
    )
    near, turn_v, twist = lax.optimization_barrier((near, turn_v, twist))
    far = lax.ppermute(near, "core", [(0, 1), (1, 0)])

    thin = min(128, rows)
    vmem = pl.BlockSpec(memory_space=pltpu.VMEM)
    gradient, weighted_residual = call(
        image_body,
        in_specs=[pl.BlockSpec(memory_space=pltpu.SMEM)] + [vmem] * 8,
        out_specs=(pl.BlockSpec(memory_space=pl.ANY), vmem),
        out_shape=(shape((rows, NPIX), f32), shape((2, n), f32)),
        scratch_shapes=[
            pltpu.VMEM((ntiles, 8, lanes), f32),
            pltpu.VMEM((8, NT * lanes + 128), f32),
            pltpu.VMEM((side, NT * lanes), bf16),
            pltpu.VMEM((2 * rows, NT * lanes), bf16),
            pltpu.VMEM((NT, side, 2 * rows), bf16),
            pltpu.VMEM((NT, 2 * side, rows), bf16),
            pltpu.VMEM((rows, NPIX), f32),
            pltpu.SemaphoreType.DMA((8,)),
            pltpu.VMEM((8, ntiles), i32),
            pltpu.SMEM((8, ntiles), i32),
        ]
        + [pltpu.VMEM((NPIX, thin), f32)] * (rows // thin),
        compiler_params=params(44),
        name="image",
    )(core.reshape(1), near, far, tile_row, rank, turn_u, rot, turn_v, twist)
    return (gradient, weighted_residual)


def solution(mesh):
    cut = mesh.devices.reshape(mesh.shape["blen"], mesh.shape["tm"] // CORES, CORES)
    whole = P(AXES)
    in_specs = (
        P(AXES, None, None, None),
        P(None, AXES),
        whole,
        whole,
        P(None, AXES),
        P(None, AXES),
        P(AXES, None),
    )
    out_specs = (P(AXES, None), P(None, AXES))
    return jax.shard_map(
        on_device, mesh=Mesh(cut, AXES), in_specs=in_specs, out_specs=out_specs, check_vma=False
    )
```

```python
import math

import jax
import jax.numpy as jnp
from jax import lax
from jax.experimental import pallas as pl
from jax.experimental.pallas import tpu as pltpu
from jax.sharding import Mesh
from jax.sharding import PartitionSpec as P

NPIX = 8192
KSUP = 8
NT = 16
TVG = 4
MOST = 4
FIELDS = 8
USED = 7
SENT = 6
CELLS = 16
CHUNK = 256

AXES = ("blen", "chip", "core")
CORES = 2
f32 = jnp.float32
bf16 = jnp.bfloat16
i32 = jnp.int32
NT_DIMS = (((1,), (1,)), ((), ()))
NN_DIMS = (((1,), (0,)), ((), ()))
MIB = 1 << 20


def params(mib):
    return pltpu.CompilerParams(vmem_limit_bytes=mib * MIB)


def split3(x):
    hi = x.astype(bf16)
    rest = x - hi.astype(f32)
    mid = rest.astype(bf16)
    low = (rest - mid.astype(f32)).astype(bf16)
    return hi, mid, low


def pattern(first, frac):
    cells = lax.broadcasted_iota(i32, (CELLS, first.shape[1]), 0)
    k = (cells - first) & (CELLS - 1)
    dist = (k - (KSUP // 2 - 1)).astype(f32) - frac
    value = jnp.where(k < KSUP, jnp.exp(-0.5 * dist * dist), 0.0).astype(bf16)
    return value, ((first + k) >> 4).astype(f32).astype(bf16)


def dense(value, where, side):
    zero = jnp.zeros_like(value)
    blocks = [jnp.where(where == jnp.bfloat16(b), value, zero) for b in range(side // CELLS)]
    return jnp.concatenate(blocks, axis=0)


def pack_body(tile_row, offset, frac, vis, weight, flag, packed, rank_out, *, devices, per_dev):
    n = tile_row.shape[1]
    t_row = tile_row[...]
    across = jnp.broadcast_to(t_row.astype(f32), (128, n)).T
    parts = []
    for c in range(n // 128):
        part = t_row[:, c * 128 : (c + 1) * 128].astype(f32)
        before = lax.broadcasted_iota(i32, (n, 128), 0)
        before = before < lax.broadcasted_iota(i32, (n, 128), 1) + c * 128
        same = jnp.where((across == part) & before, 1.0, 0.0)
        parts.append(jnp.sum(same, axis=0, keepdims=True))
    rank = jnp.concatenate(parts, axis=1).astype(i32)
    rank_out[...] = rank
    owner = t_row // per_dev
    local = t_row - owner * per_dev
    owners = lax.broadcasted_iota(i32, (devices, n), 0) == owner
    places = MOST * per_dev
    hot = lax.broadcasted_iota(i32, (places, n), 0) == rank * per_dev + local
    hot = hot.astype(f32).astype(bf16)
    rows = [
        offset[0:1, :].astype(f32),
        offset[1:2, :].astype(f32),
        frac[0:1, :],
        frac[1:2, :],
        vis[0:1, :],
        vis[1:2, :],
        weight[...] * flag[...].astype(f32),
    ]
    packed[...] = jnp.zeros(packed.shape, f32)
    for f in range(USED):
        spread = jnp.where(owners, rows[f], 0.0)
        total = jnp.zeros((devices, places), f32)
        for part in split3(spread):
            total = total + lax.dot_general(part, hot, NT_DIMS, preferred_element_type=f32)
        for k in range(MOST):
            at = (k * FIELDS + f) * per_dev
            packed[:, 0, at : at + per_dev] = total[:, k * per_dev : (k + 1) * per_dev]


def predict_body(recv, model, sent, back, fields, flip, *, per_dev):
    group = model.shape[0]
    side = model.shape[2]
    lanes = sent.shape[1]
    devices = recv.shape[0]
    step = pl.program_id(0)

    @pl.when(step == 0)
    def _():
        turned = recv[...].T
        span = FIELDS * per_dev
        for k in range(MOST):
            some = turned[k * span : (k + 1) * span, :]
            for t in range(per_dev):
                for f in range(FIELDS):
                    at = f * per_dev + t
                    fields[t, f : f + 1, k * devices : (k + 1) * devices] = some[at : at + 1, :]

    for i in range(group):
        l = step * group + i
        rows = fields[l]
        first = rows[0:2].astype(i32) - (KSUP // 2 - 1)
        ku = dense(*pattern(first[0:1], rows[2:3]), side)
        kv = dense(*pattern(first[1:2], rows[3:4]), side).astype(f32)
        for c in range(2):
            product = lax.dot_general(model[i, c], ku, NN_DIMS, preferred_element_type=f32)
            predicted = jnp.sum(product * kv, axis=0, keepdims=True)
            fields[l, 4 + c : 5 + c, :] = rows[6:7] * (predicted - rows[4 + c : 5 + c])

    @pl.when(step == per_dev // group - 1)
    def _():
        above = lax.broadcasted_iota(i32, (lanes, lanes), 0)
        above = above < lax.broadcasted_iota(i32, (lanes, lanes), 1)
        above = above.astype(f32).astype(bf16)
        there = jnp.concatenate([fields[t, 0:1, :] for t in range(per_dev)], axis=0) > 0.5
        place = lax.dot_general(
            there.astype(f32).astype(bf16), above, NN_DIMS, preferred_element_type=f32
        )
        place = jnp.where(there, place, -1.0).astype(i32)
        for t in range(per_dev):
            move = lax.broadcasted_iota(i32, (lanes, lanes), 0) == place[t : t + 1]
            move = move.astype(f32).astype(bf16)
            parts = jnp.concatenate(split3(fields[t]), axis=0)
            total = lax.dot_general(parts, move, NT_DIMS, preferred_element_type=f32)
            total = total[0:8] + total[8:16] + total[16:24]
            sent[t * SENT : (t + 1) * SENT, :] = total[0:SENT]
        mine = [fields[t, 4 + c : 5 + c, :] for c in range(2) for t in range(per_dev)]
        wide = 2 * per_dev
        flip[:, 0:wide] = jnp.concatenate(mine, axis=0).T
        back[...] = jnp.zeros(back.shape, f32)
        for core in range(CORES):
            for k in range(MOST):
                some = flip[pl.ds(k * devices + core, devices // CORES, stride=CORES), :]
                at = (core * MOST + k) * wide
                back[:, at : at + wide] = some[:, 0:wide]


def fft_pos(z):
    n = len(z)
    if n == 1:
        return z
    even = fft_pos(z[0::2])
    odd = fft_pos(z[1::2])
    low, high = [], []
    for k in range(n // 2):
        o_re, o_im = odd[k]
        if k == 0:
            t_re, t_im = o_re, o_im
        elif 4 * k == n:
            t_re, t_im = -o_im, o_re
        else:
            c, s = math.cos(2 * math.pi * k / n), math.sin(2 * math.pi * k / n)
            t_re = o_re * c - o_im * s
            t_im = o_re * s + o_im * c
        e_re, e_im = even[k]
        low.append((e_re + t_re, e_im + t_im))
        high.append((e_re - t_re, e_im - t_im))
    return low + high


def image_body(
    core, near, far, tile_row, rank, turn_u, rot, turn_v, twist, out, own,
    tiles, merged, kv_all, up_all, grid, turned, stage, sems, tally, counts, fill, *flips,
):
    side = turn_u.shape[1]
    rows2 = turn_u.shape[0]
    rows = rows2 // 2
    chips = near.shape[0]
    lanes = near.shape[2]
    per_dev = near.shape[1] // SENT
    width = flips[0].shape[1]
    most = NT * lanes // CHUNK

    there = []
    for far_off, recv in enumerate((near, far)):
        from_core = core[0] if far_off == 0 else 1 - core[0]
        for l in range(per_dev):
            some = recv[:, l * SENT : (l + 1) * SENT, :]
            filled = some[:, 0:1, :] > 0.5
            owner = lax.broadcasted_iota(i32, filled.shape, 0) * CORES + from_core
            mark = jnp.where(filled, ((owner * per_dev + l) // TVG % NT).astype(f32), 0.0)
            cells = jnp.concatenate([some, mark, jnp.zeros_like(mark)], axis=1)
            tiles[(far_off * per_dev + l) * chips : (far_off * per_dev + l + 1) * chips] = cells
            there.append(jnp.where(filled[:, 0], 1.0, 0.0).astype(bf16))
    there = jnp.concatenate(there, axis=0)
    total = lax.dot_general(
        jnp.ones((8, lanes), bf16),
        there,
        NT_DIMS,
        preferred_element_type=f32,
    )
    tally[...] = total.astype(i32)
    count_copy = pltpu.make_async_copy(tally, counts, sems.at[0])
    count_copy.start()

    n = tile_row.shape[1]
    t_row = tile_row[...]
    owner = t_row // per_dev
    local = t_row - owner * per_dev
    span = MOST * 2 * per_dev
    total = jnp.zeros((3 * lanes, n), f32)
    for far_off, recv in enumerate((near, far)):
        from_core = core[0] if far_off == 0 else 1 - core[0]
        hot = lax.broadcasted_iota(i32, (chips, n), 0) * CORES + from_core == owner
        hot = hot.astype(f32).astype(bf16)
        mine = jnp.concatenate(split3(recv[:, per_dev * SENT, :].T), axis=0)
        total = total + lax.dot_general(mine, hot, NN_DIMS, preferred_element_type=f32)
    total = total[0:lanes] + total[lanes : 2 * lanes] + total[2 * lanes : 3 * lanes]
    places = lax.broadcasted_iota(i32, (lanes, n), 0)
    for c in range(2):
        picked = places == core[0] * span + (rank[...] * 2 + c) * per_dev + local
        own[c : c + 1, :] = jnp.sum(jnp.where(picked, total, 0.0), axis=0, keepdims=True)
    count_copy.wait()

    def chunk(slot, at):
        m = merged[slot, :, pl.ds(at, CHUNK)]
        first = m[0:2].astype(i32) - (KSUP // 2 - 1)
        ku = dense(*pattern(first[0:1], m[2:3]), side)
        kv_all[:, pl.ds(at, CHUNK)] = dense(*pattern(first[1:2], m[3:4]), side)
        v = lax.dot_general(turn_u[...], ku, NN_DIMS, preferred_element_type=f32)
        r_re = m[4:5] * (1.0 / NPIX)
        r_im = m[5:6] * (1.0 / NPIX)
        which = lax.broadcasted_iota(i32, (NT, CHUNK), 0).astype(f32) == m[6:7]
        which = which.astype(f32).astype(bf16)
        which = jnp.concatenate([which] * 3, axis=0)
        turn = lax.dot_general(rot[...], which, NN_DIMS, preferred_element_type=f32)
        cos_t, sin_t = turn[:NT], turn[NT:]
        c_re = (r_re * cos_t - r_im * sin_t)[None]
        c_im = (r_re * sin_t + r_im * cos_t)[None]
        v = v.reshape(rows // NT, 2, NT, CHUNK)
        v_re, v_im = v[:, 0], v[:, 1]
        u_re = (c_re * v_re - c_im * v_im).reshape(rows, CHUNK)
        u_im = (c_re * v_im + c_im * v_re).reshape(rows, CHUNK)
        up_all[0:rows, pl.ds(at, CHUNK)] = u_re.astype(bf16)
        up_all[rows:rows2, pl.ds(at, CHUNK)] = u_im.astype(bf16)

    def product(at, size):
        return lax.dot_general(
            kv_all[:, pl.ds(at, size)],
            up_all[:, pl.ds(at, size)],
            NT_DIMS,
            preferred_element_type=f32,
        )

    def merge(tv, slot):
        group = (tv >> 2) * (NT * TVG) + (tv & 3)
        merged[slot] = jnp.zeros(merged.shape[1:], f32)
        used = jnp.int32(0)
        for tu in range(NT):
            tile = group + tu * TVG
            owner = tile >> (per_dev.bit_length() - 1)
            local = tile & (per_dev - 1)
            far_off = (owner ^ core[0]) & 1
            index = (far_off * per_dev + local) * chips + (owner >> 1)
            cell = jnp.concatenate([tiles[index], jnp.zeros((8, 128), f32)], axis=1)
            at = pl.ds(pl.multiple_of((used >> 7) << 7, 128), lanes + 128)
            merged[slot, :, at] = merged[slot, :, at] + pltpu.roll(cell, used & 127, axis=1)
            used = used + counts[0, index]
        fill[slot] = used

    def tile_column(tv, carry):
        slot = tv & 1
        following = jnp.minimum(tv + 1, NT - 1)
        chunks = (fill[slot] + CHUNK - 1) // CHUNK

        if most == 8:
            low = -1
            for n in (2, 4, 5, 6, 8):

                @pl.when((chunks > low) & (chunks <= n))
                def _():
                    for i in range(n):
                        chunk(slot, i * CHUNK)
                    merge(following, 1 - slot)
                    grid[tv] = product(0, n * CHUNK).astype(bf16)

                low = n
        else:

            def make(i, c):
                chunk(slot, pl.multiple_of(i * CHUNK, CHUNK))
                return c

            def add(i, ft):
                return ft + product(pl.multiple_of(i * CHUNK, CHUNK), CHUNK)

            lax.fori_loop(0, chunks, make, 0)
            merge(following, 1 - slot)
            ft = lax.fori_loop(0, chunks, add, jnp.zeros((side, rows2), f32))
            grid[tv] = ft.astype(bf16)
        return carry

    merge(jnp.int32(0), 0)
    lax.fori_loop(0, NT, tile_column, 0)

    def stripe(j, carry):
        r0 = pl.multiple_of(j * 16, 16)
        tc = twist[0, pl.ds(r0, 16), :]
        ts = twist[1, pl.ds(r0, 16), :]
        for h in range(rows // width):
            c0 = h * width
            z = [
                (
                    grid[t, pl.ds(r0, 16), c0 : c0 + width].astype(f32),
                    grid[t, pl.ds(r0, 16), rows + c0 : rows + c0 + width].astype(f32),
                )
                for t in range(NT)
            ]
            x = fft_pos(z)
            for n0 in range(NT):
                re, im = x[n0]
                if n0 > 0:
                    c = tc[:, n0 : n0 + 1]
                    s = ts[:, n0 : n0 + 1]
                    re, im = re * c - im * s, re * s + im * c
                turned[n0, pl.ds(r0, 16), c0 : c0 + width] = re.astype(bf16)
                turned[n0, pl.ds(r0 + side, 16), c0 : c0 + width] = im.astype(bf16)
        return carry

    lax.fori_loop(0, side // 16, stripe, 0)

    for n0 in range(NT):
        x = lax.dot_general(turn_v[...], turned[n0], NN_DIMS, preferred_element_type=f32)
        for h in range(rows // width):
            flips[h][pl.ds(n0, side, stride=NT), :] = x[:, h * width : (h + 1) * width]

    pieces = sems.shape[0]
    wide = NPIX // pieces
    copies = []
    for i in range(pieces):
        for h in range(rows // width):
            stage[h * width : (h + 1) * width, i * wide : (i + 1) * wide] = (
                flips[h][i * wide : (i + 1) * wide, :].T
            )
        copy = pltpu.make_async_copy(
            stage.at[:, pl.ds(i * wide, wide)], out.at[:, pl.ds(i * wide, wide)], sems.at[i]
        )
        copy.start()
        copies.append(copy)
    for copy in copies:
        copy.wait()


def cos_sin(product, period):
    angle = (2.0 * math.pi / period) * (product % period).astype(f32)
    return jnp.cos(angle), jnp.sin(angle)


def on_device(model_grid, vis_values, weights, flags, uv_frac, cell_offset, tile_index):
    chips = lax.axis_size("blen") * lax.axis_size("chip")
    devices = chips * CORES
    core = lax.axis_index("core")
    me = (lax.axis_index("blen") * lax.axis_size("chip") + lax.axis_index("chip")) * CORES + core
    per_dev = model_grid.shape[0]
    side = model_grid.shape[2]
    n = weights.shape[0]
    ntiles = per_dev * devices
    lanes = devices * MOST
    rows = NPIX // devices
    call = pl.pallas_call
    shape = jax.ShapeDtypeStruct

    tile_row = tile_index.reshape(1, n)
    width = MOST * FIELDS * per_dev
    packed, rank = call(
        lambda *refs: pack_body(*refs, devices=devices, per_dev=per_dev),
        out_shape=(shape((devices, 1, width), f32), shape((1, n), i32)),
        name="pack",
    )(tile_row, cell_offset, uv_frac, vis_values, weights.reshape(1, n), flags.reshape(1, n))
    recv = lax.all_to_all(packed, AXES, split_axis=0, concat_axis=0, tiled=True)
    recv = recv.reshape(devices, width)
    image_rows = me * rows + jnp.arange(rows, dtype=i32)
    cells = jnp.arange(side, dtype=i32)
    small = jnp.arange(NT, dtype=i32)
    turn_u = cos_sin((image_rows[:, None] * cells[None, :]).reshape(rows // NT, NT, side), NPIX)
    turn_u = jnp.stack(turn_u, axis=1).reshape(2 * rows, side).astype(bf16)
    rot = cos_sin(small[:, None] * small[None, :], NT)
    rot = jnp.concatenate(split3(jnp.concatenate(rot)), axis=1)
    cos_v, sin_v = cos_sin(cells[:, None] * cells[None, :], side)
    turn_v = jnp.concatenate([cos_v, -sin_v], axis=1).astype(bf16)
    twist = jnp.stack(cos_sin(cells[:, None] * small[None, :], NPIX))
    recv, turn_u, rot, twist = lax.optimization_barrier((recv, turn_u, rot, twist))

    group = min(2, per_dev)
    sent, back = call(
        lambda *refs: predict_body(*refs, per_dev=per_dev),
        grid=(per_dev // group,),
        in_specs=[
            pl.BlockSpec((devices, width), lambda l: (0, 0)),
            pl.BlockSpec((group, 2, side, side), lambda l: (l, 0, 0, 0)),
        ],
        out_specs=(
            pl.BlockSpec((per_dev * SENT, lanes), lambda l: (0, 0)),
            pl.BlockSpec((chips, lanes), lambda l: (0, 0)),
        ),
        out_shape=(shape((per_dev * SENT, lanes), f32), shape((chips, lanes), f32)),
        scratch_shapes=[pltpu.VMEM((per_dev, FIELDS, lanes), f32), pltpu.VMEM((lanes, 128), f32)],
        compiler_params=params(32),
        name="predict",
    )(recv, pltpu.with_memory_space_constraint(model_grid, pltpu.HBM))
    sent = jnp.broadcast_to(sent[None], (chips,) + sent.shape)
    near = lax.all_to_all(
        jnp.concatenate([sent, back[:, None, :]], axis=1),
        AXES[:2],
        split_axis=0,
        concat_axis=0,
        tiled=True,
    )
    near, turn_v, twist = lax.optimization_barrier((near, turn_v, twist))
    far = lax.ppermute(near, "core", [(0, 1), (1, 0)])

    thin = min(128, rows)
    vmem = pl.BlockSpec(memory_space=pltpu.VMEM)
    gradient, weighted_residual = call(
        image_body,
        in_specs=[pl.BlockSpec(memory_space=pltpu.SMEM)] + [vmem] * 8,
        out_specs=(pl.BlockSpec(memory_space=pl.ANY), vmem),
        out_shape=(shape((rows, NPIX), f32), shape((2, n), f32)),
        scratch_shapes=[
            pltpu.VMEM((ntiles, 8, lanes), f32),
            pltpu.VMEM((2, 8, NT * lanes + 128), f32),
            pltpu.VMEM((side, NT * lanes), bf16),
            pltpu.VMEM((2 * rows, NT * lanes), bf16),
            pltpu.VMEM((NT, side, 2 * rows), bf16),
            pltpu.VMEM((NT, 2 * side, rows), bf16),
            pltpu.VMEM((rows, NPIX), f32),
            pltpu.SemaphoreType.DMA((8,)),
            pltpu.VMEM((8, ntiles), i32),
            pltpu.SMEM((8, ntiles), i32),
            pltpu.SMEM((2,), i32),
        ]
        + [pltpu.VMEM((NPIX, thin), f32)] * (rows // thin),
        compiler_params=params(44),
        name="image",
    )(core.reshape(1), near, far, tile_row, rank, turn_u, rot, turn_v, twist)
    return (gradient, weighted_residual)


def solution(mesh):
    cut = mesh.devices.reshape(mesh.shape["blen"], mesh.shape["tm"] // CORES, CORES)
    whole = P(AXES)
    in_specs = (
        P(AXES, None, None, None),
        P(None, AXES),
        whole,
        whole,
        P(None, AXES),
        P(None, AXES),
        P(AXES, None),
    )
    out_specs = (P(AXES, None), P(None, AXES))
    return jax.shard_map(
        on_device, mesh=Mesh(cut, AXES), in_specs=in_specs, out_specs=out_specs, check_vma=False
    )
```

```python
import math

import jax
import jax.numpy as jnp
from jax import lax
from jax.experimental import pallas as pl
from jax.experimental.pallas import tpu as pltpu
from jax.sharding import Mesh
from jax.sharding import PartitionSpec as P

NPIX = 8192
KSUP = 8
NT = 16
TVG = 4
MOST = 4
FIELDS = 8
USED = 7
SENT = 6
CELLS = 16
CHUNK = 256
PARTS = 4

AXES = ("blen", "chip", "core")
CORES = 2
f32 = jnp.float32
bf16 = jnp.bfloat16
i32 = jnp.int32
NT_DIMS = (((1,), (1,)), ((), ()))
NN_DIMS = (((1,), (0,)), ((), ()))
MIB = 1 << 20


def params(mib):
    return pltpu.CompilerParams(vmem_limit_bytes=mib * MIB)


def split3(x):
    hi = x.astype(bf16)
    rest = x - hi.astype(f32)
    mid = rest.astype(bf16)
    low = (rest - mid.astype(f32)).astype(bf16)
    return hi, mid, low


def pattern(first, frac):
    cells = lax.broadcasted_iota(i32, (CELLS, first.shape[1]), 0)
    k = (cells - first) & (CELLS - 1)
    dist = (k - (KSUP // 2 - 1)).astype(f32) - frac
    value = jnp.where(k < KSUP, jnp.exp(-0.5 * dist * dist), 0.0).astype(bf16)
    return value, ((first + k) >> 4).astype(f32).astype(bf16)


def dense(value, where, side):
    zero = jnp.zeros_like(value)
    blocks = [jnp.where(where == jnp.bfloat16(b), value, zero) for b in range(side // CELLS)]
    return jnp.concatenate(blocks, axis=0)


def pack_body(tile_row, offset, frac, vis, weight, flag, packed, rank_out, *, devices, per_dev):
    n = tile_row.shape[1]
    t_row = tile_row[...]
    across = jnp.broadcast_to(t_row.astype(f32), (128, n)).T
    parts = []
    for c in range(n // 128):
        part = t_row[:, c * 128 : (c + 1) * 128].astype(f32)
        before = lax.broadcasted_iota(i32, (n, 128), 0)
        before = before < lax.broadcasted_iota(i32, (n, 128), 1) + c * 128
        same = jnp.where((across == part) & before, 1.0, 0.0)
        parts.append(jnp.sum(same, axis=0, keepdims=True))
    rank = jnp.concatenate(parts, axis=1).astype(i32)
    rank_out[...] = rank
    owner = t_row // per_dev
    local = t_row - owner * per_dev
    owners = lax.broadcasted_iota(i32, (devices, n), 0) == owner
    places = MOST * per_dev
    hot = lax.broadcasted_iota(i32, (places, n), 0) == rank * per_dev + local
    hot = hot.astype(f32).astype(bf16)
    rows = [
        offset[0:1, :].astype(f32),
        offset[1:2, :].astype(f32),
        frac[0:1, :],
        frac[1:2, :],
        vis[0:1, :],
        vis[1:2, :],
        weight[...] * flag[...].astype(f32),
    ]
    packed[...] = jnp.zeros(packed.shape, f32)
    for f in range(USED):
        spread = jnp.where(owners, rows[f], 0.0)
        total = jnp.zeros((devices, places), f32)
        for part in split3(spread):
            total = total + lax.dot_general(part, hot, NT_DIMS, preferred_element_type=f32)
        for k in range(MOST):
            at = (k * FIELDS + f) * per_dev
            packed[:, 0, at : at + per_dev] = total[:, k * per_dev : (k + 1) * per_dev]


def predict_body(recv, model, sent, back, fields, flip, *, per_dev):
    group = model.shape[0]
    side = model.shape[2]
    lanes = sent.shape[1]
    devices = recv.shape[0]
    step = pl.program_id(0)

    @pl.when(step == 0)
    def _():
        turned = recv[...].T
        span = FIELDS * per_dev
        lined = [turned[k * span : (k + 1) * span, :] for k in range(MOST)]
        lined = jnp.concatenate(lined, axis=1)
        for f in range(FIELDS):
            fields[:, f, :] = lined[f * per_dev : (f + 1) * per_dev, :]

    for i in range(group):
        l = step * group + i
        rows = fields[l]
        first = rows[0:2].astype(i32) - (KSUP // 2 - 1)
        ku = dense(*pattern(first[0:1], rows[2:3]), side)
        kv = dense(*pattern(first[1:2], rows[3:4]), side).astype(f32)
        for c in range(2):
            product = lax.dot_general(model[i, c], ku, NN_DIMS, preferred_element_type=f32)
            predicted = jnp.sum(product * kv, axis=0, keepdims=True)
            fields[l, 4 + c : 5 + c, :] = rows[6:7] * (predicted - rows[4 + c : 5 + c])

    @pl.when(step == per_dev // group - 1)
    def _():
        above = lax.broadcasted_iota(i32, (lanes, lanes), 0)
        above = above < lax.broadcasted_iota(i32, (lanes, lanes), 1)
        above = above.astype(f32).astype(bf16)
        there = jnp.concatenate([fields[t, 0:1, :] for t in range(per_dev)], axis=0) > 0.5
        place = lax.dot_general(
            there.astype(f32).astype(bf16), above, NN_DIMS, preferred_element_type=f32
        )
        place = jnp.where(there, place, -1.0).astype(i32)
        for t in range(per_dev):
            move = lax.broadcasted_iota(i32, (lanes, lanes), 0) == place[t : t + 1]
            move = move.astype(f32).astype(bf16)
            parts = jnp.concatenate(split3(fields[t]), axis=0)
            total = lax.dot_general(parts, move, NT_DIMS, preferred_element_type=f32)
            total = total[0:8] + total[8:16] + total[16:24]
            sent[t * SENT : (t + 1) * SENT, :] = total[0:SENT]
        mine = [fields[t, 4 + c : 5 + c, :] for c in range(2) for t in range(per_dev)]
        wide = 2 * per_dev
        flip[:, 0:wide] = jnp.concatenate(mine, axis=0).T
        back[...] = jnp.zeros(back.shape, f32)
        for core in range(CORES):
            for k in range(MOST):
                some = flip[pl.ds(k * devices + core, devices // CORES, stride=CORES), :]
                at = (core * MOST + k) * wide
                back[:, at : at + wide] = some[:, 0:wide]


def fft_pos(z):
    n = len(z)
    if n == 1:
        return z
    even = fft_pos(z[0::2])
    odd = fft_pos(z[1::2])
    low, high = [], []
    for k in range(n // 2):
        o_re, o_im = odd[k]
        if k == 0:
            t_re, t_im = o_re, o_im
        elif 4 * k == n:
            t_re, t_im = -o_im, o_re
        else:
            c, s = math.cos(2 * math.pi * k / n), math.sin(2 * math.pi * k / n)
            t_re = o_re * c - o_im * s
            t_im = o_re * s + o_im * c
        e_re, e_im = even[k]
        low.append((e_re + t_re, e_im + t_im))
        high.append((e_re - t_re, e_im - t_im))
    return low + high


def image_body(
    core, near, far, tile_row, rank, turn_u, rot, turn_v, twist, out, own,
    tiles, merged, kv_all, up_all, grid, turned, stage, sems, tally, counts, fill, *flips,
):
    side = turn_u.shape[1]
    rows2 = turn_u.shape[0]
    rows = rows2 // 2
    chips = near.shape[0]
    lanes = near.shape[2]
    per_dev = near.shape[1] // SENT
    width = flips[0].shape[1]
    most = NT * lanes // CHUNK

    there = []
    for far_off, recv in enumerate((near, far)):
        from_core = core[0] if far_off == 0 else 1 - core[0]
        for l in range(per_dev):
            some = recv[:, l * SENT : (l + 1) * SENT, :]
            filled = some[:, 0:1, :] > 0.5
            owner = lax.broadcasted_iota(i32, filled.shape, 0) * CORES + from_core
            mark = jnp.where(filled, ((owner * per_dev + l) // TVG % NT).astype(f32), 0.0)
            cells = jnp.concatenate([some, mark, jnp.zeros_like(mark)], axis=1)
            tiles[(far_off * per_dev + l) * chips : (far_off * per_dev + l + 1) * chips] = cells
            there.append(jnp.where(filled[:, 0], 1.0, 0.0).astype(bf16))
    there = jnp.concatenate(there, axis=0)
    total = lax.dot_general(
        jnp.ones((8, lanes), bf16),
        there,
        NT_DIMS,
        preferred_element_type=f32,
    )
    tally[...] = total.astype(i32)
    count_copy = pltpu.make_async_copy(tally, counts, sems.at[0])
    count_copy.start()

    n = tile_row.shape[1]
    t_row = tile_row[...]
    owner = t_row // per_dev
    local = t_row - owner * per_dev
    span = MOST * 2 * per_dev
    total = jnp.zeros((3 * lanes, n), f32)
    for far_off, recv in enumerate((near, far)):
        from_core = core[0] if far_off == 0 else 1 - core[0]
        hot = lax.broadcasted_iota(i32, (chips, n), 0) * CORES + from_core == owner
        hot = hot.astype(f32).astype(bf16)
        mine = jnp.concatenate(split3(recv[:, per_dev * SENT, :].T), axis=0)
        total = total + lax.dot_general(mine, hot, NN_DIMS, preferred_element_type=f32)
    total = total[0:lanes] + total[lanes : 2 * lanes] + total[2 * lanes : 3 * lanes]
    places = lax.broadcasted_iota(i32, (lanes, n), 0)
    for c in range(2):
        picked = places == core[0] * span + (rank[...] * 2 + c) * per_dev + local
        own[c : c + 1, :] = jnp.sum(jnp.where(picked, total, 0.0), axis=0, keepdims=True)
    count_copy.wait()

    def chunk(slot, at):
        m = merged[slot, :, pl.ds(at, CHUNK)]
        first = m[0:2].astype(i32) - (KSUP // 2 - 1)
        ku = dense(*pattern(first[0:1], m[2:3]), side)
        kv_all[:, pl.ds(at, CHUNK)] = dense(*pattern(first[1:2], m[3:4]), side)
        v = lax.dot_general(turn_u[...], ku, NN_DIMS, preferred_element_type=f32)
        r_re = m[4:5] * (1.0 / NPIX)
        r_im = m[5:6] * (1.0 / NPIX)
        which = lax.broadcasted_iota(i32, (NT, CHUNK), 0).astype(f32) == m[6:7]
        which = which.astype(f32).astype(bf16)
        which = jnp.concatenate([which] * 3, axis=0)
        turn = lax.dot_general(rot[...], which, NN_DIMS, preferred_element_type=f32)
        cos_t, sin_t = turn[:NT], turn[NT:]
        c_re = (r_re * cos_t - r_im * sin_t)[None]
        c_im = (r_re * sin_t + r_im * cos_t)[None]
        v = v.reshape(rows // NT, 2, NT, CHUNK)
        v_re, v_im = v[:, 0], v[:, 1]
        u_re = (c_re * v_re - c_im * v_im).reshape(rows, CHUNK)
        u_im = (c_re * v_im + c_im * v_re).reshape(rows, CHUNK)
        up_all[0:rows, pl.ds(at, CHUNK)] = u_re.astype(bf16)
        up_all[rows:rows2, pl.ds(at, CHUNK)] = u_im.astype(bf16)

    def product(at, size):
        return lax.dot_general(
            kv_all[:, pl.ds(at, size)],
            up_all[:, pl.ds(at, size)],
            NT_DIMS,
            preferred_element_type=f32,
        )

    def merge(tv, slot):
        group = (tv >> 2) * (NT * TVG) + (tv & 3)
        merged[slot] = jnp.zeros(merged.shape[1:], f32)
        used = jnp.int32(0)
        for tu in range(NT):
            tile = group + tu * TVG
            owner = tile >> (per_dev.bit_length() - 1)
            local = tile & (per_dev - 1)
            far_off = (owner ^ core[0]) & 1
            index = (far_off * per_dev + local) * chips + (owner >> 1)
            cell = jnp.concatenate([tiles[index], jnp.zeros((8, 128), f32)], axis=1)
            at = pl.ds(pl.multiple_of((used >> 7) << 7, 128), lanes + 128)
            merged[slot, :, at] = merged[slot, :, at] + pltpu.roll(cell, used & 127, axis=1)
            used = used + counts[0, index]
        fill[slot] = used

    def tile_column(tv, carry):
        slot = tv & 1
        following = jnp.minimum(tv + 1, NT - 1)
        chunks = (fill[slot] + CHUNK - 1) // CHUNK

        if most == 8:
            low = -1
            for n in (2, 4, 5, 6, 8):

                @pl.when((chunks > low) & (chunks <= n))
                def _():
                    for i in range(n):
                        chunk(slot, i * CHUNK)
                    merge(following, 1 - slot)
                    grid[tv] = product(0, n * CHUNK).astype(bf16)

                low = n
        else:

            def make(i, c):
                chunk(slot, pl.multiple_of(i * CHUNK, CHUNK))
                return c

            def add(i, ft):
                return ft + product(pl.multiple_of(i * CHUNK, CHUNK), CHUNK)

            lax.fori_loop(0, chunks, make, 0)
            merge(following, 1 - slot)
            ft = lax.fori_loop(0, chunks, add, jnp.zeros((side, rows2), f32))
            grid[tv] = ft.astype(bf16)
        return carry

    merge(jnp.int32(0), 0)
    lax.fori_loop(0, NT, tile_column, 0)

    def stripe(j, carry):
        r0 = pl.multiple_of(j * 16, 16)
        tc = twist[0, pl.ds(r0, 16), :]
        ts = twist[1, pl.ds(r0, 16), :]
        for h in range(rows // width):
            c0 = h * width
            z = [
                (
                    grid[t, pl.ds(r0, 16), c0 : c0 + width].astype(f32),
                    grid[t, pl.ds(r0, 16), rows + c0 : rows + c0 + width].astype(f32),
                )
                for t in range(NT)
            ]
            x = fft_pos(z)
            for n0 in range(NT):
                re, im = x[n0]
                if n0 > 0:
                    c = tc[:, n0 : n0 + 1]
                    s = ts[:, n0 : n0 + 1]
                    re, im = re * c - im * s, re * s + im * c
                turned[n0, pl.ds(r0, 16), c0 : c0 + width] = re.astype(bf16)
                turned[n0, pl.ds(r0 + side, 16), c0 : c0 + width] = im.astype(bf16)
        return carry

    lax.fori_loop(0, side // 16, stripe, 0)

    pieces = sems.shape[0]
    wide = NPIX // pieces
    copies = []
    part = side // PARTS
    for b in range(PARTS):
        for n0 in range(NT):
            x = lax.dot_general(
                turn_v[b * part : (b + 1) * part, :],
                turned[n0],
                NN_DIMS,
                preferred_element_type=f32,
            )
            for h in range(rows // width):
                flips[h][pl.ds(b * part * NT + n0, part, stride=NT), :] = (
                    x[:, h * width : (h + 1) * width]
                )
        for i in range(b * pieces // PARTS, (b + 1) * pieces // PARTS):
            for h in range(rows // width):
                stage[h * width : (h + 1) * width, i * wide : (i + 1) * wide] = (
                    flips[h][i * wide : (i + 1) * wide, :].T
                )
            copy = pltpu.make_async_copy(
                stage.at[:, pl.ds(i * wide, wide)], out.at[:, pl.ds(i * wide, wide)], sems.at[i]
            )
            copy.start()
            copies.append(copy)
    for copy in copies:
        copy.wait()


def cos_sin(product, period):
    angle = (2.0 * math.pi / period) * (product % period).astype(f32)
    return jnp.cos(angle), jnp.sin(angle)


def on_device(model_grid, vis_values, weights, flags, uv_frac, cell_offset, tile_index):
    chips = lax.axis_size("blen") * lax.axis_size("chip")
    devices = chips * CORES
    core = lax.axis_index("core")
    me = (lax.axis_index("blen") * lax.axis_size("chip") + lax.axis_index("chip")) * CORES + core
    per_dev = model_grid.shape[0]
    side = model_grid.shape[2]
    n = weights.shape[0]
    ntiles = per_dev * devices
    lanes = devices * MOST
    rows = NPIX // devices
    call = pl.pallas_call
    shape = jax.ShapeDtypeStruct

    tile_row = tile_index.reshape(1, n)
    width = MOST * FIELDS * per_dev
    packed, rank = call(
        lambda *refs: pack_body(*refs, devices=devices, per_dev=per_dev),
        out_shape=(shape((devices, 1, width), f32), shape((1, n), i32)),
        name="pack",
    )(tile_row, cell_offset, uv_frac, vis_values, weights.reshape(1, n), flags.reshape(1, n))
    recv = lax.all_to_all(packed, AXES, split_axis=0, concat_axis=0, tiled=True)
    recv = recv.reshape(devices, width)
    image_rows = me * rows + jnp.arange(rows, dtype=i32)
    cells = jnp.arange(side, dtype=i32)
    small = jnp.arange(NT, dtype=i32)
    turn_u = cos_sin((image_rows[:, None] * cells[None, :]).reshape(rows // NT, NT, side), NPIX)
    turn_u = jnp.stack(turn_u, axis=1).reshape(2 * rows, side).astype(bf16)
    rot = cos_sin(small[:, None] * small[None, :], NT)
    rot = jnp.concatenate(split3(jnp.concatenate(rot)), axis=1)
    cos_v, sin_v = cos_sin(cells[:, None] * cells[None, :], side)
    turn_v = jnp.concatenate([cos_v, -sin_v], axis=1).astype(bf16)
    twist = jnp.stack(cos_sin(cells[:, None] * small[None, :], NPIX))
    recv, turn_u, rot, twist = lax.optimization_barrier((recv, turn_u, rot, twist))

    group = min(4, per_dev)
    sent, back = call(
        lambda *refs: predict_body(*refs, per_dev=per_dev),
        grid=(per_dev // group,),
        in_specs=[
            pl.BlockSpec((devices, width), lambda l: (0, 0)),
            pl.BlockSpec((group, 2, side, side), lambda l: (l, 0, 0, 0)),
        ],
        out_specs=(
            pl.BlockSpec((per_dev * SENT, lanes), lambda l: (0, 0)),
            pl.BlockSpec((chips, lanes), lambda l: (0, 0)),
        ),
        out_shape=(shape((per_dev * SENT, lanes), f32), shape((chips, lanes), f32)),
        scratch_shapes=[pltpu.VMEM((per_dev, FIELDS, lanes), f32), pltpu.VMEM((lanes, 128), f32)],
        compiler_params=params(32),
        name="predict",
    )(recv, pltpu.with_memory_space_constraint(model_grid, pltpu.HBM))
    sent = jnp.broadcast_to(sent[None], (chips,) + sent.shape)
    near = lax.all_to_all(
        jnp.concatenate([sent, back[:, None, :]], axis=1),
        AXES[:2],
        split_axis=0,
        concat_axis=0,
        tiled=True,
    )
    near, turn_v, twist = lax.optimization_barrier((near, turn_v, twist))
    far = lax.ppermute(near, "core", [(0, 1), (1, 0)])

    thin = min(128, rows)
    vmem = pl.BlockSpec(memory_space=pltpu.VMEM)
    gradient, weighted_residual = call(
        image_body,
        in_specs=[pl.BlockSpec(memory_space=pltpu.SMEM)] + [vmem] * 8,
        out_specs=(pl.BlockSpec(memory_space=pl.ANY), vmem),
        out_shape=(shape((rows, NPIX), f32), shape((2, n), f32)),
        scratch_shapes=[
            pltpu.VMEM((ntiles, 8, lanes), f32),
            pltpu.VMEM((2, 8, NT * lanes + 128), f32),
            pltpu.VMEM((side, NT * lanes), bf16),
            pltpu.VMEM((2 * rows, NT * lanes), bf16),
            pltpu.VMEM((NT, side, 2 * rows), bf16),
            pltpu.VMEM((NT, 2 * side, rows), bf16),
            pltpu.VMEM((rows, NPIX), f32),
            pltpu.SemaphoreType.DMA((8,)),
            pltpu.VMEM((8, ntiles), i32),
            pltpu.SMEM((8, ntiles), i32),
            pltpu.SMEM((2,), i32),
        ]
        + [pltpu.VMEM((NPIX, thin), f32)] * (rows // thin),
        compiler_params=params(44),
        name="image",
    )(core.reshape(1), near, far, tile_row, rank, turn_u, rot, turn_v, twist)
    return (gradient, weighted_residual)


def solution(mesh):
    cut = mesh.devices.reshape(mesh.shape["blen"], mesh.shape["tm"] // CORES, CORES)
    whole = P(AXES)
    in_specs = (
        P(AXES, None, None, None),
        P(None, AXES),
        whole,
        whole,
        P(None, AXES),
        P(None, AXES),
        P(AXES, None),
    )
    out_specs = (P(AXES, None), P(None, AXES))
    return jax.shard_map(
        on_device, mesh=Mesh(cut, AXES), in_specs=in_specs, out_specs=out_specs, check_vma=False
    )
```

```python
import math

import jax
import jax.numpy as jnp
from jax import lax
from jax.experimental import pallas as pl
from jax.experimental.pallas import tpu as pltpu
from jax.sharding import Mesh
from jax.sharding import PartitionSpec as P

NPIX = 8192
KSUP = 8
NT = 16
TVG = 4
MOST = 4
FIELDS = 8
USED = 7
SENT = 6
CELLS = 16
CHUNK = 256
PARTS = 8

AXES = ("blen", "chip", "core")
CORES = 2
f32 = jnp.float32
bf16 = jnp.bfloat16
i32 = jnp.int32
NT_DIMS = (((1,), (1,)), ((), ()))
NN_DIMS = (((1,), (0,)), ((), ()))
MIB = 1 << 20


def params(mib):
    return pltpu.CompilerParams(vmem_limit_bytes=mib * MIB)


def split3(x):
    hi = x.astype(bf16)
    rest = x - hi.astype(f32)
    mid = rest.astype(bf16)
    low = (rest - mid.astype(f32)).astype(bf16)
    return hi, mid, low


def pattern(first, frac):
    cells = lax.broadcasted_iota(i32, (CELLS, first.shape[1]), 0)
    k = (cells - first) & (CELLS - 1)
    dist = (k - (KSUP // 2 - 1)).astype(f32) - frac
    value = jnp.where(k < KSUP, jnp.exp(-0.5 * dist * dist), 0.0).astype(bf16)
    return value, ((first + k) >> 4).astype(f32).astype(bf16)


def dense(value, where, side):
    zero = jnp.zeros_like(value)
    blocks = [jnp.where(where == jnp.bfloat16(b), value, zero) for b in range(side // CELLS)]
    return jnp.concatenate(blocks, axis=0)


def pack_body(tile_row, offset, frac, vis, weight, flag, packed, rank_out, *, devices, per_dev):
    n = tile_row.shape[1]
    t_row = tile_row[...]
    across = jnp.broadcast_to(t_row.astype(f32), (128, n)).T
    parts = []
    for c in range(n // 128):
        part = t_row[:, c * 128 : (c + 1) * 128].astype(f32)
        before = lax.broadcasted_iota(i32, (n, 128), 0)
        before = before < lax.broadcasted_iota(i32, (n, 128), 1) + c * 128
        same = jnp.where((across == part) & before, 1.0, 0.0)
        parts.append(jnp.sum(same, axis=0, keepdims=True))
    rank = jnp.concatenate(parts, axis=1).astype(i32)
    rank_out[...] = rank
    owner = t_row // per_dev
    local = t_row - owner * per_dev
    owners = lax.broadcasted_iota(i32, (devices, n), 0) == owner
    places = MOST * per_dev
    hot = lax.broadcasted_iota(i32, (places, n), 0) == rank * per_dev + local
    hot = hot.astype(f32).astype(bf16)
    rows = [
        offset[0:1, :].astype(f32),
        offset[1:2, :].astype(f32),
        frac[0:1, :],
        frac[1:2, :],
        vis[0:1, :],
        vis[1:2, :],
        weight[...] * flag[...].astype(f32),
    ]
    packed[...] = jnp.zeros(packed.shape, f32)
    for f in range(USED):
        spread = jnp.where(owners, rows[f], 0.0)
        total = jnp.zeros((devices, places), f32)
        for part in split3(spread):
            total = total + lax.dot_general(part, hot, NT_DIMS, preferred_element_type=f32)
        for k in range(MOST):
            at = (k * FIELDS + f) * per_dev
            packed[:, 0, at : at + per_dev] = total[:, k * per_dev : (k + 1) * per_dev]


def predict_body(recv, model, sent, back, fields, flip, *, per_dev):
    group = model.shape[0]
    side = model.shape[2]
    lanes = sent.shape[1]
    devices = recv.shape[0]
    step = pl.program_id(0)

    @pl.when(step == 0)
    def _():
        turned = recv[...].T
        span = FIELDS * per_dev
        lined = [turned[k * span : (k + 1) * span, :] for k in range(MOST)]
        lined = jnp.concatenate(lined, axis=1)
        for f in range(FIELDS):
            fields[:, f, :] = lined[f * per_dev : (f + 1) * per_dev, :]

    for i in range(group):
        l = step * group + i
        rows = fields[l]
        first = rows[0:2].astype(i32) - (KSUP // 2 - 1)
        ku = dense(*pattern(first[0:1], rows[2:3]), side)
        kv = dense(*pattern(first[1:2], rows[3:4]), side).astype(f32)
        for c in range(2):
            product = lax.dot_general(model[i, c], ku, NN_DIMS, preferred_element_type=f32)
            predicted = jnp.sum(product * kv, axis=0, keepdims=True)
            fields[l, 4 + c : 5 + c, :] = rows[6:7] * (predicted - rows[4 + c : 5 + c])

    @pl.when(step == per_dev // group - 1)
    def _():
        above = lax.broadcasted_iota(i32, (lanes, lanes), 0)
        above = above < lax.broadcasted_iota(i32, (lanes, lanes), 1)
        above = above.astype(f32).astype(bf16)
        there = jnp.concatenate([fields[t, 0:1, :] for t in range(per_dev)], axis=0) > 0.5
        place = lax.dot_general(
            there.astype(f32).astype(bf16), above, NN_DIMS, preferred_element_type=f32
        )
        place = jnp.where(there, place, -1.0).astype(i32)
        for t in range(per_dev):
            move = lax.broadcasted_iota(i32, (lanes, lanes), 0) == place[t : t + 1]
            move = move.astype(f32).astype(bf16)
            parts = jnp.concatenate(split3(fields[t]), axis=0)
            total = lax.dot_general(parts, move, NT_DIMS, preferred_element_type=f32)
            total = total[0:8] + total[8:16] + total[16:24]
            sent[t * SENT : (t + 1) * SENT, :] = total[0:SENT]
        mine = [fields[t, 4 + c : 5 + c, :] for c in range(2) for t in range(per_dev)]
        wide = 2 * per_dev
        flip[:, 0:wide] = jnp.concatenate(mine, axis=0).T
        back[...] = jnp.zeros(back.shape, f32)
        for core in range(CORES):
            for k in range(MOST):
                some = flip[pl.ds(k * devices + core, devices // CORES, stride=CORES), :]
                at = (core * MOST + k) * wide
                back[:, at : at + wide] = some[:, 0:wide]


def fft_pos(z):
    n = len(z)
    if n == 1:
        return z
    even = fft_pos(z[0::2])
    odd = fft_pos(z[1::2])
    low, high = [], []
    for k in range(n // 2):
        o_re, o_im = odd[k]
        if k == 0:
            t_re, t_im = o_re, o_im
        elif 4 * k == n:
            t_re, t_im = -o_im, o_re
        else:
            c, s = math.cos(2 * math.pi * k / n), math.sin(2 * math.pi * k / n)
            t_re = o_re * c - o_im * s
            t_im = o_re * s + o_im * c
        e_re, e_im = even[k]
        low.append((e_re + t_re, e_im + t_im))
        high.append((e_re - t_re, e_im - t_im))
    return low + high


def image_body(
    core, near, far, tile_row, rank, turn_u, rot, turn_v, twist, out, own,
    tiles, merged, kv_all, up_all, grid, turned, stage, sems, tally, counts, fill, *flips,
):
    side = turn_u.shape[1]
    rows2 = turn_u.shape[0]
    rows = rows2 // 2
    chips = near.shape[0]
    lanes = near.shape[2]
    per_dev = near.shape[1] // SENT
    width = flips[0].shape[1]
    most = NT * lanes // CHUNK

    there = []
    for far_off, recv in enumerate((near, far)):
        from_core = core[0] if far_off == 0 else 1 - core[0]
        for l in range(per_dev):
            some = recv[:, l * SENT : (l + 1) * SENT, :]
            filled = some[:, 0:1, :] > 0.5
            owner = lax.broadcasted_iota(i32, filled.shape, 0) * CORES + from_core
            mark = jnp.where(filled, ((owner * per_dev + l) // TVG % NT).astype(f32), 0.0)
            cells = jnp.concatenate([some, mark, jnp.zeros_like(mark)], axis=1)
            tiles[(far_off * per_dev + l) * chips : (far_off * per_dev + l + 1) * chips] = cells
            there.append(jnp.where(filled[:, 0], 1.0, 0.0).astype(bf16))
    there = jnp.concatenate(there, axis=0)
    total = lax.dot_general(
        jnp.ones((8, lanes), bf16),
        there,
        NT_DIMS,
        preferred_element_type=f32,
    )
    tally[...] = total.astype(i32)
    count_copy = pltpu.make_async_copy(tally, counts, sems.at[0])
    count_copy.start()

    n = tile_row.shape[1]
    t_row = tile_row[...]
    owner = t_row // per_dev
    local = t_row - owner * per_dev
    span = MOST * 2 * per_dev
    total = jnp.zeros((3 * lanes, n), f32)
    for far_off, recv in enumerate((near, far)):
        from_core = core[0] if far_off == 0 else 1 - core[0]
        hot = lax.broadcasted_iota(i32, (chips, n), 0) * CORES + from_core == owner
        hot = hot.astype(f32).astype(bf16)
        mine = jnp.concatenate(split3(recv[:, per_dev * SENT, :].T), axis=0)
        total = total + lax.dot_general(mine, hot, NN_DIMS, preferred_element_type=f32)
    total = total[0:lanes] + total[lanes : 2 * lanes] + total[2 * lanes : 3 * lanes]
    places = lax.broadcasted_iota(i32, (lanes, n), 0)
    for c in range(2):
        picked = places == core[0] * span + (rank[...] * 2 + c) * per_dev + local
        own[c : c + 1, :] = jnp.sum(jnp.where(picked, total, 0.0), axis=0, keepdims=True)
    count_copy.wait()

    def chunk(slot, at):
        m = merged[slot, :, pl.ds(at, CHUNK)]
        first = m[0:2].astype(i32) - (KSUP // 2 - 1)
        ku = dense(*pattern(first[0:1], m[2:3]), side)
        kv_all[:, pl.ds(at, CHUNK)] = dense(*pattern(first[1:2], m[3:4]), side)
        v = lax.dot_general(turn_u[...], ku, NN_DIMS, preferred_element_type=f32)
        r_re = m[4:5] * (1.0 / NPIX)
        r_im = m[5:6] * (1.0 / NPIX)
        which = lax.broadcasted_iota(i32, (NT, CHUNK), 0).astype(f32) == m[6:7]
        which = which.astype(f32).astype(bf16)
        which = jnp.concatenate([which] * 3, axis=0)
        turn = lax.dot_general(rot[...], which, NN_DIMS, preferred_element_type=f32)
        cos_t, sin_t = turn[:NT], turn[NT:]
        c_re = (r_re * cos_t - r_im * sin_t)[None]
        c_im = (r_re * sin_t + r_im * cos_t)[None]
        v = v.reshape(rows // NT, 2, NT, CHUNK)
        v_re, v_im = v[:, 0], v[:, 1]
        u_re = (c_re * v_re - c_im * v_im).reshape(rows, CHUNK)
        u_im = (c_re * v_im + c_im * v_re).reshape(rows, CHUNK)
        up_all[0:rows, pl.ds(at, CHUNK)] = u_re.astype(bf16)
        up_all[rows:rows2, pl.ds(at, CHUNK)] = u_im.astype(bf16)

    def product(at, size):
        return lax.dot_general(
            kv_all[:, pl.ds(at, size)],
            up_all[:, pl.ds(at, size)],
            NT_DIMS,
            preferred_element_type=f32,
        )

    def merge(tv, slot):
        group = (tv >> 2) * (NT * TVG) + (tv & 3)
        merged[slot] = jnp.zeros(merged.shape[1:], f32)
        used = jnp.int32(0)
        for tu in range(NT):
            tile = group + tu * TVG
            owner = tile >> (per_dev.bit_length() - 1)
            local = tile & (per_dev - 1)
            far_off = (owner ^ core[0]) & 1
            index = (far_off * per_dev + local) * chips + (owner >> 1)
            cell = jnp.concatenate([tiles[index], jnp.zeros((8, 128), f32)], axis=1)
            at = pl.ds(pl.multiple_of((used >> 7) << 7, 128), lanes + 128)
            merged[slot, :, at] = merged[slot, :, at] + pltpu.roll(cell, used & 127, axis=1)
            used = used + counts[0, index]
        fill[slot] = used

    def tile_column(tv, carry):
        slot = tv & 1
        following = jnp.minimum(tv + 1, NT - 1)
        chunks = (fill[slot] + CHUNK - 1) // CHUNK

        if most == 8:
            low = -1
            for n in (2, 4, 5, 6, 8):

                @pl.when((chunks > low) & (chunks <= n))
                def _():
                    for i in range(n):
                        chunk(slot, i * CHUNK)
                    merge(following, 1 - slot)
                    grid[tv] = product(0, n * CHUNK).astype(bf16)

                low = n
        else:

            def make(i, c):
                chunk(slot, pl.multiple_of(i * CHUNK, CHUNK))
                return c

            def add(i, ft):
                return ft + product(pl.multiple_of(i * CHUNK, CHUNK), CHUNK)

            lax.fori_loop(0, chunks, make, 0)
            merge(following, 1 - slot)
            ft = lax.fori_loop(0, chunks, add, jnp.zeros((side, rows2), f32))
            grid[tv] = ft.astype(bf16)
        return carry

    merge(jnp.int32(0), 0)
    lax.fori_loop(0, NT, tile_column, 0)

    def stripe(j, carry):
        r0 = pl.multiple_of(j * 16, 16)
        tc = twist[0, pl.ds(r0, 16), :]
        ts = twist[1, pl.ds(r0, 16), :]
        for h in range(rows // width):
            c0 = h * width
            z = [
                (
                    grid[t, pl.ds(r0, 16), c0 : c0 + width].astype(f32),
                    grid[t, pl.ds(r0, 16), rows + c0 : rows + c0 + width].astype(f32),
                )
                for t in range(NT)
            ]
            x = fft_pos(z)
            for n0 in range(NT):
                re, im = x[n0]
                if n0 > 0:
                    c = tc[:, n0 : n0 + 1]
                    s = ts[:, n0 : n0 + 1]
                    re, im = re * c - im * s, re * s + im * c
                turned[n0, pl.ds(r0, 16), c0 : c0 + width] = re.astype(bf16)
                turned[n0, pl.ds(r0 + side, 16), c0 : c0 + width] = im.astype(bf16)
        return carry

    lax.fori_loop(0, side // 16, stripe, 0)

    pieces = sems.shape[0]
    wide = NPIX // pieces
    copies = []
    part = side // PARTS
    for b in range(PARTS):
        for n0 in range(NT):
            x = lax.dot_general(
                turn_v[b * part : (b + 1) * part, :],
                turned[n0],
                NN_DIMS,
                preferred_element_type=f32,
            )
            for h in range(rows // width):
                flips[h][pl.ds(b * part * NT + n0, part, stride=NT), :] = (
                    x[:, h * width : (h + 1) * width]
                )
        for i in range(b * pieces // PARTS, (b + 1) * pieces // PARTS):
            for h in range(rows // width):
                stage[h * width : (h + 1) * width, i * wide : (i + 1) * wide] = (
                    flips[h][i * wide : (i + 1) * wide, :].T
                )
            copy = pltpu.make_async_copy(
                stage.at[:, pl.ds(i * wide, wide)], out.at[:, pl.ds(i * wide, wide)], sems.at[i]
            )
            copy.start()
            copies.append(copy)
    for copy in copies:
        copy.wait()


def cos_sin(product, period):
    angle = (2.0 * math.pi / period) * (product % period).astype(f32)
    return jnp.cos(angle), jnp.sin(angle)


def on_device(model_grid, vis_values, weights, flags, uv_frac, cell_offset, tile_index):
    chips = lax.axis_size("blen") * lax.axis_size("chip")
    devices = chips * CORES
    core = lax.axis_index("core")
    me = (lax.axis_index("blen") * lax.axis_size("chip") + lax.axis_index("chip")) * CORES + core
    per_dev = model_grid.shape[0]
    side = model_grid.shape[2]
    n = weights.shape[0]
    ntiles = per_dev * devices
    lanes = devices * MOST
    rows = NPIX // devices
    call = pl.pallas_call
    shape = jax.ShapeDtypeStruct

    tile_row = tile_index.reshape(1, n)
    width = MOST * FIELDS * per_dev
    packed, rank = call(
        lambda *refs: pack_body(*refs, devices=devices, per_dev=per_dev),
        out_shape=(shape((devices, 1, width), f32), shape((1, n), i32)),
        name="pack",
    )(tile_row, cell_offset, uv_frac, vis_values, weights.reshape(1, n), flags.reshape(1, n))
    recv = lax.all_to_all(packed, AXES, split_axis=0, concat_axis=0, tiled=True)
    recv = recv.reshape(devices, width)
    image_rows = me * rows + jnp.arange(rows, dtype=i32)
    cells = jnp.arange(side, dtype=i32)
    small = jnp.arange(NT, dtype=i32)
    turn_u = cos_sin((image_rows[:, None] * cells[None, :]).reshape(rows // NT, NT, side), NPIX)
    turn_u = jnp.stack(turn_u, axis=1).reshape(2 * rows, side).astype(bf16)
    rot = cos_sin(small[:, None] * small[None, :], NT)
    rot = jnp.concatenate(split3(jnp.concatenate(rot)), axis=1)
    cos_v, sin_v = cos_sin(cells[:, None] * cells[None, :], side)
    turn_v = jnp.concatenate([cos_v, -sin_v], axis=1).astype(bf16)
    twist = jnp.stack(cos_sin(cells[:, None] * small[None, :], NPIX))
    recv, turn_u, rot, twist = lax.optimization_barrier((recv, turn_u, rot, twist))

    group = min(4, per_dev)
    sent, back = call(
        lambda *refs: predict_body(*refs, per_dev=per_dev),
        grid=(per_dev // group,),
        in_specs=[
            pl.BlockSpec((devices, width), lambda l: (0, 0)),
            pl.BlockSpec((group, 2, side, side), lambda l: (l, 0, 0, 0)),
        ],
        out_specs=(
            pl.BlockSpec((per_dev * SENT, lanes), lambda l: (0, 0)),
            pl.BlockSpec((chips, lanes), lambda l: (0, 0)),
        ),
        out_shape=(shape((per_dev * SENT, lanes), f32), shape((chips, lanes), f32)),
        scratch_shapes=[pltpu.VMEM((per_dev, FIELDS, lanes), f32), pltpu.VMEM((lanes, 128), f32)],
        compiler_params=params(32),
        name="predict",
    )(recv, pltpu.with_memory_space_constraint(model_grid, pltpu.HBM))
    sent = jnp.broadcast_to(sent[None], (chips,) + sent.shape)
    near = lax.all_to_all(
        jnp.concatenate([sent, back[:, None, :]], axis=1),
        AXES[:2],
        split_axis=0,
        concat_axis=0,
        tiled=True,
    )
    near, turn_v, twist = lax.optimization_barrier((near, turn_v, twist))
    far = lax.ppermute(near, "core", [(0, 1), (1, 0)])

    thin = min(128, rows)
    vmem = pl.BlockSpec(memory_space=pltpu.VMEM)
    gradient, weighted_residual = call(
        image_body,
        in_specs=[pl.BlockSpec(memory_space=pltpu.SMEM)] + [vmem] * 8,
        out_specs=(pl.BlockSpec(memory_space=pl.ANY), vmem),
        out_shape=(shape((rows, NPIX), f32), shape((2, n), f32)),
        scratch_shapes=[
            pltpu.VMEM((ntiles, 8, lanes), f32),
            pltpu.VMEM((2, 8, NT * lanes + 128), f32),
            pltpu.VMEM((side, NT * lanes), bf16),
            pltpu.VMEM((2 * rows, NT * lanes), bf16),
            pltpu.VMEM((NT, side, 2 * rows), bf16),
            pltpu.VMEM((NT, 2 * side, rows), bf16),
            pltpu.VMEM((rows, NPIX), f32),
            pltpu.SemaphoreType.DMA((8,)),
            pltpu.VMEM((8, ntiles), i32),
            pltpu.SMEM((8, ntiles), i32),
            pltpu.SMEM((2,), i32),
        ]
        + [pltpu.VMEM((NPIX, thin), f32)] * (rows // thin),
        compiler_params=params(44),
        name="image",
    )(core.reshape(1), near, far, tile_row, rank, turn_u, rot, turn_v, twist)
    return (gradient, weighted_residual)


def solution(mesh):
    cut = mesh.devices.reshape(mesh.shape["blen"], mesh.shape["tm"] // CORES, CORES)
    whole = P(AXES)
    in_specs = (
        P(AXES, None, None, None),
        P(None, AXES),
        whole,
        whole,
        P(None, AXES),
        P(None, AXES),
        P(AXES, None),
    )
    out_specs = (P(AXES, None), P(None, AXES))
    return jax.shard_map(
        on_device, mesh=Mesh(cut, AXES), in_specs=in_specs, out_specs=out_specs, check_vma=False
    )
```
